256 devices in a mesh: grp: 8 (over y, core), seq: 32 (over x, z).
Axes of the slice: x: 4, y: 4, z: 8, core: 2. Of those that a mesh axis runs over, the one named last changes fastest.
Arguments:
- queries: float32 [262144, 256], P(('grp', 'seq')), may hold values from -6 to 6
- keys: float32 [262144, 256], P(('grp', 'seq')), may hold values from -6 to 6
- values: float32 [262144, 256], P(('grp', 'seq')), may hold values from -6 to 6
Outputs:
- mixed: float32 [262144, 256], P(('grp', 'seq'))
The draws below stay inside these ranges and needn't reach their ends.
All inputs are finite; a program needn't handle non-finite values.
Results may differ from the reference program's by a relative error of at most 0.00018.
Values sent between devices are 32-bit elements; how exact they have to be, the bound alone decides.
A program may use at most 192 MiB of HBM per device.

```python
import math
import jax
import jax.numpy as jnp
from jax import lax

HEADS = 2
HEAD = 128
BLOCK = 256
ITERS = 4
TOK_DEV = 1024
TOKENS = 262144


def draw_keys(key, part):
    width = HEADS * HEAD
    scales = jnp.exp(jax.random.uniform(jax.random.fold_in(key, 11), (width,), jnp.float32, math.log(0.2), 0.0))
    base = jax.random.truncated_normal(jax.random.fold_in(key, 13), -6.0, 6.0, (TOKENS, width), jnp.float32)
    return (base * scales).astype(jnp.float32)


def level_of(stream_key, extent, cuts, smallest, largest):
    gain, own = 1.0, jax.random.fold_in(stream_key, 6)
    for position, shards_of in cuts:
        heights = jnp.exp(jax.random.uniform(jax.random.fold_in(own, position), (shards_of,), jnp.float32, smallest / len(cuts), largest / len(cuts)))
        gain = gain * jnp.repeat(heights, extent[position] // shards_of).reshape([-1 if axis == position else 1 for axis in range(len(extent))])
    return gain


def scatter_about(key, extent, deviation, reach, shards=(), held_as=jnp.bfloat16):
    values = jax.random.normal(key, extent, jnp.float32) * deviation
    if len(shards) > 0:
        values = level_of(key, extent, shards, -0.22, 0.18) * values
    return jnp.clip(values, min=-reach, max=reach).astype(held_as)


def setup_inputs(seed: int = 0) -> dict:
    arg_keys = jax.random.split(jax.random.key(seed), 4)
    return {
        "queries": scatter_about(arg_keys[0], (TOKENS, HEADS * HEAD), 1.0, 6.0, ((0, 256),), jnp.float32),
        "keys": draw_keys(jax.random.fold_in(arg_keys[3], 71), 0),
        "values": scatter_about(arg_keys[2], (TOKENS, HEADS * HEAD), 1.0, 6.0, ((0, 256),), jnp.float32),
    }


ridge = 1.0

def block_solve(qb, kb, vb, gram_pre, vk_pre):
    size = qb.shape[2]
    rows = lax.broadcasted_iota(jnp.int32, (size, size), 0)
    cols = lax.broadcasted_iota(jnp.int32, (size, size), 1)
    causal = (cols <= rows).astype(jnp.float32)
    best = lax.Precision.HIGHEST

    def apply(direc):
        own = jnp.einsum('hnta,hnab->hntb', direc, gram_pre, precision=best)
        scores = jnp.einsum('hnta,hnsa->hnts', direc, kb, precision=best) * causal
        return own + jnp.einsum('hnts,hnsb->hntb', scores, kb, precision=best) + ridge * direc
    solved = jnp.zeros_like(qb)
    resid = qb
    direc = qb
    norm_now = lax.optimization_barrier(jnp.sum(resid * resid, axis=-1, keepdims=True))
    for step in range(ITERS):
        image = apply(direc)
        alpha = norm_now / lax.optimization_barrier(jnp.sum(direc * image, axis=-1, keepdims=True))
        solved = solved + alpha * direc
        resid = resid - alpha * image
        norm_next = lax.optimization_barrier(jnp.sum(resid * resid, axis=-1, keepdims=True))
        direc = resid + norm_next / norm_now * direc
        norm_now = norm_next
    outer = jnp.einsum('hntb,hnab->hnta', solved, vk_pre, precision=best)
    scores = jnp.einsum('hntb,hnsb->hnts', solved, kb, precision=best) * causal
    return outer + jnp.einsum('hnts,hnsa->hnta', scores, vb, precision=best)

def exclusive_sum(blocks):
    summed = jnp.cumsum(blocks, axis=1)
    return jnp.concatenate([jnp.zeros_like(blocks[:, :1]), summed[:, :-1]], axis=1)

def reference(queries, keys, values):
    total = queries.shape[0]
    count = total // BLOCK
    best = lax.Precision.HIGHEST

    def split(arr):
        return arr.reshape(count, BLOCK, HEADS, HEAD).transpose(2, 0, 1, 3)
    qb, kb, vb = (split(queries), split(keys), split(values))
    gram_blk = jnp.einsum('hnsa,hnsb->hnab', kb, kb, precision=best)
    vk_blk = jnp.einsum('hnsa,hnsb->hnab', vb, kb, precision=best)
    gram_pre = exclusive_sum(gram_blk)
    vk_pre = exclusive_sum(vk_blk)
    per = TOK_DEV // BLOCK
    groups = count // per

    def regroup(arr):
        shaped = arr.reshape((HEADS, groups, per) + arr.shape[2:])
        return jnp.moveaxis(shaped, 1, 0)

    def work(items):
        return block_solve(items[0], items[1], items[2], items[3], items[4])
    outs = lax.map(work, (regroup(qb), regroup(kb), regroup(vb), regroup(gram_pre), regroup(vk_pre)))
    outs = jnp.moveaxis(outs, 0, 1).reshape(HEADS, count, BLOCK, HEAD)
    mixed = outs.transpose(1, 2, 0, 3).reshape(total, HEADS * HEAD)
    place = jnp.arange(total, dtype=jnp.int32).astype(jnp.float32)
    return mixed * jnp.sqrt(place + 1.0)[:, None]
```

```python
import functools

import jax
import jax.numpy as jnp
from jax import lax
from jax.experimental import pallas as pl
from jax.experimental.pallas import tpu as pltpu
from jax.sharding import PartitionSpec as P

HEADS = 2
HEAD = 128
BLOCK = 256
ITERS = 4
ZDIM = 8
F32 = jnp.float32
BF16 = jnp.bfloat16
MESH = pl.DeviceIdType.MESH


def halves(x):
    hi = x.astype(BF16)
    return hi, (x - hi.astype(F32)).astype(BF16)


def mm(a, b):
    return jnp.dot(a, b, preferred_element_type=F32)


def mmt(a, b):
    return lax.dot_general(a, b, (((0,), (0,)), ((), ())), preferred_element_type=F32)


def block_sums(k, v):
    k_hi, k_lo = halves(k)
    v_hi, v_lo = halves(v)
    wide = mmt(k_hi, jnp.concatenate([k_hi, k_lo, v_hi, v_lo], axis=1))
    rest = mmt(k_lo, jnp.concatenate([k_hi, v_hi], axis=1))
    gram = wide[:, :HEAD] + wide[:, HEAD : 2 * HEAD] + rest[:, :HEAD]
    state = wide[:, 2 * HEAD : 3 * HEAD] + wide[:, 3 * HEAD :] + rest[:, HEAD:]
    return gram, state


def scan_kernel(
    nz, k_hbm, v_hbm, e_ref, loc_hbm,
    kbuf, vbuf, loc, sums, zin, zpre, xin, gin, eout,
    ksem, vsem, locsem, zs, zr, xs, xr, gs, gr, es, er,
):
    g, s = lax.axis_index("grp"), lax.axis_index("seq")
    ng, nx = lax.axis_size("grp"), lax.axis_size("seq") // nz
    z, x = s % nz, s // nz
    blocks = kbuf.shape[0] // BLOCK
    rows = sums.shape[1]

    def along_z(d):
        return {"grp": g, "seq": x * nz + (z + d) % nz}

    def along_x(d):
        return {"grp": g, "seq": ((x + d) % nx) * nz + z}

    def along_g(d):
        return {"grp": (g + d) % ng, "seq": s}

    barrier = pltpu.get_barrier_semaphore()
    loads = []
    for b in range(blocks):
        at = pl.ds(b * BLOCK, BLOCK)
        loads.append((
            pltpu.make_async_copy(k_hbm.at[at], kbuf.at[at], ksem.at[b]),
            pltpu.make_async_copy(v_hbm.at[at], vbuf.at[at], vsem.at[b]),
        ))
        loads[-1][0].start()
        loads[-1][1].start()
    partners = [along_z(d) for d in range(1, nz)] + [along_x(d) for d in range(1, nx)] + [along_g(d) for d in range(1, ng)]
    for partner in partners:
        pl.semaphore_signal(barrier, inc=1, device_id=partner, device_id_type=MESH)

    total = [jnp.zeros((HEAD, HEAD), F32) for _ in range(2 * HEADS)]
    for b in range(blocks):
        loads[b][0].wait()
        loads[b][1].wait()
        for h in range(HEADS):
            at = (pl.ds(b * BLOCK, BLOCK), pl.ds(h * HEAD, HEAD))
            pair = block_sums(kbuf[at], vbuf[at])
            for i in range(2):
                loc[b, pl.ds((2 * h + i) * HEAD, HEAD), :] = total[2 * h + i]
                total[2 * h + i] = total[2 * h + i] + pair[i]
    per = HEAD // rows
    for i in range(2 * HEADS):
        sums[pl.ds(i * per, per)] = total[i].reshape(per, rows, HEAD)
    out_loc = pltpu.make_async_copy(loc, loc_hbm, locsem)
    out_loc.start()

    pl.semaphore_wait(barrier, len(partners))

    def zcopy(d):
        return pltpu.make_async_remote_copy(
            src_ref=sums.at[(z + d) % nz], dst_ref=zin.at[z], send_sem=zs.at[d], recv_sem=zr.at[d],
            device_id=along_z(d), device_id_type=MESH)

    def xcopy(d):
        return pltpu.make_async_remote_copy(
            src_ref=xin.at[x], dst_ref=xin.at[x], send_sem=xs.at[d], recv_sem=xr.at[d],
            device_id=along_x(d), device_id_type=MESH)

    def gcopy(d):
        return pltpu.make_async_remote_copy(
            src_ref=gin.at[g], dst_ref=gin.at[g], send_sem=gs.at[d], recv_sem=gr.at[d],
            device_id=along_g(d), device_id_type=MESH)

    def ecopy(d):
        return pltpu.make_async_remote_copy(
            src_ref=eout.at[(z + d) % nz], dst_ref=e_ref.at[z], send_sem=es.at[d], recv_sem=er.at[d],
            device_id=along_z(d), device_id_type=MESH)

    far_first = sorted(range(1, nz), key=lambda d: -min(d, nz - d))
    for d in far_first:
        zcopy(d).start()
    zin[z] = sums[z]
    for d in range(1, nz):
        zcopy(d).wait_recv()
    run = jnp.zeros((rows, HEAD), F32)
    for j in range(nz):
        zpre[j] = run
        run = run + zin[j]

    xin[x] = run
    for d in range(1, nx):
        xcopy(d).start()
    for d in range(1, nx):
        xcopy(d).wait_recv()
    before, whole = jnp.zeros((rows, HEAD), F32), jnp.zeros((rows, HEAD), F32)
    for j in range(nx):
        piece = xin[j]
        before = before + jnp.where(j < x, piece, 0.0)
        whole = whole + piece

    gin[g] = whole
    for d in range(1, ng):
        @pl.when(g + d < ng)
        def _():
            gcopy(d).start()
    for d in range(1, ng):
        @pl.when(g - d >= 0)
        def _():
            gcopy(d).wait_recv()
    before = before + lax.fori_loop(0, g, lambda j, acc: acc + gin[j], jnp.zeros((rows, HEAD), F32))

    for j in range(nz):
        eout[j] = zpre[j] + before
    for d in far_first:
        ecopy(d).start()
    e_ref[z] = eout[z]
    for d in range(1, nz):
        zcopy(d).wait_send()
    for d in range(1, nx):
        xcopy(d).wait_send()
    for d in range(1, ng):
        @pl.when(g + d < ng)
        def _():
            gcopy(d).wait_send()
    out_loc.wait()
    for d in range(1, nz):
        ecopy(d).wait_send()
        ecopy(d).wait_recv()


def entering(keys, values, nz):
    rows_local, width = keys.shape
    blocks = rows_local // BLOCK
    nx, ng = lax.axis_size("seq") // nz, lax.axis_size("grp")
    rows = 2 * HEADS * HEAD // nz
    any_space = pl.BlockSpec(memory_space=pl.ANY)
    dma = pltpu.SemaphoreType.DMA
    e, loc = pl.pallas_call(
        functools.partial(scan_kernel, nz),
        out_shape=(
            jax.ShapeDtypeStruct((nz, rows, HEAD), F32),
            jax.ShapeDtypeStruct((blocks, 2 * HEADS * HEAD, HEAD), F32),
        ),
        in_specs=[any_space, any_space],
        out_specs=(pl.BlockSpec(memory_space=pltpu.VMEM), any_space),
        scratch_shapes=[
            pltpu.VMEM((rows_local, width), F32),
            pltpu.VMEM((rows_local, width), F32),
            pltpu.VMEM((blocks, 2 * HEADS * HEAD, HEAD), F32),
            pltpu.VMEM((nz, rows, HEAD), F32),
            pltpu.VMEM((nz, rows, HEAD), F32),
            pltpu.VMEM((nz, rows, HEAD), F32),
            pltpu.VMEM((nx, rows, HEAD), F32),
            pltpu.VMEM((ng, rows, HEAD), F32),
            pltpu.VMEM((nz, rows, HEAD), F32),
            dma((blocks,)), dma((blocks,)), dma,
            dma((nz,)), dma((nz,)), dma((nx,)), dma((nx,)), dma((ng,)), dma((ng,)), dma((nz,)), dma((nz,)),
        ],
        compiler_params=pltpu.CompilerParams(collective_id=0, has_side_effects=True),
        name="scan",
    )(keys, values)
    return e.reshape(2 * HEADS * HEAD, HEAD), loc


def solve_kernel(q_ref, k_ref, v_ref, e_ref, loc_ref, out_ref):
    rows = lax.broadcasted_iota(jnp.int32, (BLOCK, BLOCK), 0)
    cols = lax.broadcasted_iota(jnp.int32, (BLOCK, BLOCK), 1)
    causal = cols <= rows
    probs = []
    for h in range(HEADS):
        lanes = pl.ds(h * HEAD, HEAD)
        q, k, v = q_ref[:, lanes], k_ref[:, lanes], v_ref[:, lanes]
        at = [pl.ds((2 * h + i) * HEAD, HEAD) for i in range(2)]
        gram = e_ref[at[0], :] + loc_ref[0, at[0], :]
        state = e_ref[at[1], :] + loc_ref[0, at[1], :]
        kt_hi, kt_lo = halves(k.T)
        gram_hi, gram_lo = halves(gram)
        state_hi, state_lo = halves(state)
        probs.append(dict(
            q=q, top=jnp.concatenate([gram_hi, kt_hi], axis=1), low=jnp.concatenate([gram_lo, kt_lo], axis=1),
            top_end=jnp.concatenate([state_hi, kt_hi], axis=1), low_end=jnp.concatenate([state_lo, kt_lo], axis=1),
            k=halves(k), v=halves(v)))

    def spread(p, top, low, right):
        p_hi, p_lo = halves(p)
        t = mm(jnp.concatenate([p_hi, p_lo], axis=1), jnp.concatenate([top, top], axis=0)) + mm(p_hi, low)
        scores = jnp.where(causal, t[:, HEAD:], 0.0)
        s_hi, s_lo = halves(scores)
        u = mm(s_hi, jnp.concatenate(right, axis=1))
        return t[:, :HEAD] + (u[:, :HEAD] + u[:, HEAD:] + mm(s_lo, right[0]))

    def dots(a, b):
        return jnp.sum(a * b, axis=-1, keepdims=True)

    state = [dict(x=jnp.zeros_like(p["q"]), r=p["q"], p=p["q"], rr=dots(p["q"], p["q"])) for p in probs]
    for step in range(ITERS):
        images = [spread(st["p"], pr["top"], pr["low"], pr["k"]) + st["p"] for st, pr in zip(state, probs)]
        for st, image in zip(state, images):
            alpha = st["rr"] / dots(st["p"], image)
            st["x"] = st["x"] + alpha * st["p"]
            if step < ITERS - 1:
                st["r"] = st["r"] - alpha * image
                new = dots(st["r"], st["r"])
                st["p"] = st["r"] + new / st["rr"] * st["p"]
                st["rr"] = new
    first = (lax.axis_index("grp") * lax.axis_size("seq") + lax.axis_index("seq")) * (pl.num_programs(0) * BLOCK)
    first = first + pl.program_id(0) * BLOCK
    place = (first + lax.broadcasted_iota(jnp.int32, (BLOCK, HEAD), 0)).astype(F32)
    scale = jnp.sqrt(place + 1.0)
    for h, (st, pr) in enumerate(zip(state, probs)):
        out_ref[:, pl.ds(h * HEAD, HEAD)] = spread(st["x"], pr["top_end"], pr["low_end"], pr["v"]) * scale


def solve(queries, keys, values, e, loc):
    rows_local, width = queries.shape
    tok = pl.BlockSpec((BLOCK, width), lambda n: (n, 0))
    return pl.pallas_call(
        solve_kernel,
        grid=(rows_local // BLOCK,),
        out_shape=jax.ShapeDtypeStruct((rows_local, width), F32),
        in_specs=[tok, tok, tok, pl.BlockSpec(e.shape, lambda n: (0, 0)), pl.BlockSpec((1,) + loc.shape[1:], lambda n: (n, 0, 0))],
        out_specs=tok,
        name="solve",
    )(queries, keys, values, e, loc)


def on_device(queries, keys, values):
    e, loc = entering(keys, values, ZDIM)
    return solve(queries, keys, values, e, loc)


def solution(mesh):
    return jax.shard_map(
        on_device,
        mesh=mesh,
        in_specs=(P(("grp", "seq"), None), P(("grp", "seq"), None), P(("grp", "seq"), None)),
        out_specs=P(("grp", "seq"), None),
        check_vma=False,
    )
```

```python
import functools

import jax
import jax.numpy as jnp
from jax import lax
from jax.experimental import pallas as pl
from jax.experimental.pallas import tpu as pltpu
from jax.sharding import PartitionSpec as P

HEADS = 2
HEAD = 128
BLOCK = 256
ITERS = 4
ZDIM = 8
GROUP = 512
CHANS = 2 * HEADS
F32 = jnp.float32
BF16 = jnp.bfloat16
MESH = pl.DeviceIdType.MESH


def halves(x):
    hi = x.astype(BF16)
    return hi, (x - hi.astype(F32)).astype(BF16)


def cat(*xs, axis):
    return jnp.concatenate(xs, axis=axis)


def mm(a, b):
    return jnp.dot(a, b, preferred_element_type=F32)


def mmt(a, b):
    return lax.dot_general(a, b, (((0,), (0,)), ((), ())), preferred_element_type=F32)


def narrow(a_hi, a_lo, b_hi, b_lo):
    right = cat(cat(b_hi, b_lo, axis=1), cat(b_hi, jnp.zeros_like(b_lo), axis=1), axis=0)
    t = mm(cat(a_hi, a_lo, axis=1), right)
    return t[:, :HEAD] + t[:, HEAD:]


def scores_of(a_hi, a_lo, kt_hi, kt_lo):
    return mm(cat(a_hi, a_lo, axis=1), cat(kt_hi, kt_hi, axis=0)) + mm(a_hi, kt_lo)


def weighted(s, b_hi, b_lo):
    s_hi, s_lo = halves(s)
    t = mm(s_hi, cat(b_hi, b_lo, axis=1))
    return t[:, :HEAD] + t[:, HEAD:] + mm(s_lo, b_hi)


def causal_mask():
    rows = lax.broadcasted_iota(jnp.int32, (BLOCK, BLOCK), 0)
    cols = lax.broadcasted_iota(jnp.int32, (BLOCK, BLOCK), 1)
    return cols <= rows


def lanes(h):
    return pl.ds(h * HEAD, HEAD)


def scan_kernel(
    nz, q_hbm, k_hbm, v_hbm, e_ref, loc_ref, q_ref, img_ref, s_ref, kt_ref, kh_ref, vh_ref,
    kbuf, vbuf, sums, zin, zpre, xin, gin, eout,
    qsem, ksem, vsem, zs, zr, xs, xr, gs, gr, es, er,
):
    g, s = lax.axis_index("grp"), lax.axis_index("seq")
    ng, nx = lax.axis_size("grp"), lax.axis_size("seq") // nz
    z, x = s % nz, s // nz
    blocks = kbuf.shape[0] // BLOCK
    rows = HEAD // nz

    def along_z(d):
        return {"grp": g, "seq": x * nz + (z + d) % nz}

    def along_x(d):
        return {"grp": g, "seq": ((x + d) % nx) * nz + z}

    def along_g(d):
        return {"grp": (g + d) % ng, "seq": s}

    loads = {}
    for h in range(HEADS):
        for b in range(blocks):
            at = (pl.ds(b * BLOCK, BLOCK), lanes(h))
            loads[h, b] = (
                pltpu.make_async_copy(k_hbm.at[at], kbuf.at[at], ksem.at[h, b]),
                pltpu.make_async_copy(v_hbm.at[at], vbuf.at[at], vsem.at[h, b]),
            )
            loads[h, b][0].start()
            loads[h, b][1].start()
    q_load = pltpu.make_async_copy(q_hbm, q_ref, qsem)
    q_load.start()
    barrier = pltpu.get_barrier_semaphore()
    partners = [along_z(d) for d in range(1, nz)] + [along_x(d) for d in range(1, nx)] + [along_g(d) for d in range(1, ng)]
    for partner in partners:
        pl.semaphore_signal(barrier, inc=1, device_id=partner, device_id_type=MESH)

    def remote(src, dst, send, recv, to):
        return pltpu.make_async_remote_copy(
            src_ref=src, dst_ref=dst, send_sem=send, recv_sem=recv, device_id=to, device_id_type=MESH)

    def zcopy(c, d):
        return remote(sums.at[c, (z + d) % nz], zin.at[c, z], zs.at[c, d], zr.at[c, d], along_z(d))

    def xcopy(c, d):
        return remote(xin.at[c, x], xin.at[c, x], xs.at[c, d], xr.at[c, d], along_x(d))

    def gcopy(c, d):
        return remote(gin.at[c, g], gin.at[c, g], gs.at[c, d], gr.at[c, d], along_g(d))

    def ecopy(c, d):
        return remote(eout.at[c, (z + d) % nz], e_ref.at[c, z], es.at[c, d], er.at[c, d], along_z(d))

    far_first = sorted(range(1, nz), key=lambda d: -min(d, nz - d))

    for h in range(HEADS):
        total = [jnp.zeros((HEAD, HEAD), F32) for _ in range(2)]
        for b in range(blocks):
            loads[h, b][0].wait()
            loads[h, b][1].wait()
            at = (pl.ds(b * BLOCK, BLOCK), lanes(h))
            k_hi, k_lo = halves(kbuf[at])
            v_hi, v_lo = halves(vbuf[at])
            kh_ref[0, b, h] = k_hi
            kh_ref[1, b, h] = k_lo
            vh_ref[0, b, h] = v_hi
            vh_ref[1, b, h] = v_lo
            wide = mmt(k_hi, cat(k_hi, k_lo, v_hi, v_lo, axis=1))
            rest = mmt(k_lo, cat(k_hi, v_hi, axis=1))
            for i in range(2):
                loc_ref[b, pl.ds((2 * h + i) * HEAD, HEAD), :] = total[i]
                base = 2 * i * HEAD
                total[i] = total[i] + (wide[:, base : base + HEAD] + wide[:, base + HEAD : base + 2 * HEAD] + rest[:, i * HEAD : (i + 1) * HEAD])
        for i in range(2):
            sums[2 * h + i] = total[i].reshape(nz, rows, HEAD)
        if h == 0:
            pl.semaphore_wait(barrier, len(partners))
        for i in range(2):
            for d in far_first:
                zcopy(2 * h + i, d).start()
            zin[2 * h + i, z] = sums[2 * h + i, z]

    q_load.wait()

    @pl.loop(0, blocks)
    def _(b):
        causal = causal_mask()
        row = pl.ds(pl.multiple_of(b * BLOCK, BLOCK), BLOCK)
        for h in range(HEADS):
            q = q_ref[row, lanes(h)]
            q_hi, q_lo = halves(q)
            kt_hi, kt_lo = halves(kbuf[row, lanes(h)].T)
            kt_ref[0, b, h] = kt_hi
            kt_ref[1, b, h] = kt_lo
            scores = jnp.where(causal, scores_of(q_hi, q_lo, kt_hi, kt_lo), 0.0)
            s_ref[b, h] = scores
            gram = halves(loc_ref[b, pl.ds(2 * h * HEAD, HEAD), :])
            near = weighted(scores, kh_ref[0, b, h], kh_ref[1, b, h])
            img_ref[row, lanes(h)] = near + narrow(q_hi, q_lo, *gram) + q

    zero = jnp.zeros((rows, HEAD), F32)
    held = {}

    def after_z(c):
        for d in range(1, nz):
            zcopy(c, d).wait_recv()
        run = zero
        for j in range(nz):
            zpre[c, j] = run
            run = run + zin[c, j]
        xin[c, x] = run
        for d in range(1, nx):
            xcopy(c, d).start()

    def after_x(c):
        for d in range(1, nx):
            xcopy(c, d).wait_recv()
        before, whole = zero, zero
        for j in range(nx):
            piece = xin[c, j]
            before = before + jnp.where(j < x, piece, 0.0)
            whole = whole + piece
        held[c] = before
        gin[c, g] = whole
        for d in range(1, ng):
            @pl.when(g + d < ng)
            def _():
                gcopy(c, d).start()

    def after_g(c):
        for d in range(1, ng):
            @pl.when(g - d >= 0)
            def _():
                gcopy(c, d).wait_recv()
        before = held[c] + lax.fori_loop(0, g, lambda j, acc: acc + gin[c, j], zero)
        for j in range(nz):
            eout[c, j] = zpre[c, j] + before
        for d in far_first:
            ecopy(c, d).start()
        e_ref[c, z] = eout[c, z]

    lag_x, lag_g = 2, 3
    for t in range(CHANS + lag_x + lag_g):
        if t < CHANS:
            after_z(t)
        if 0 <= t - lag_x < CHANS:
            after_x(t - lag_x)
        if 0 <= t - lag_x - lag_g < CHANS:
            after_g(t - lag_x - lag_g)

    for c in range(CHANS):
        for d in range(1, nz):
            zcopy(c, d).wait_send()
        for d in range(1, nx):
            xcopy(c, d).wait_send()
        for d in range(1, ng):
            @pl.when(g + d < ng)
            def _():
                gcopy(c, d).wait_send()
    for c in range(CHANS):
        for d in range(1, nz):
            ecopy(c, d).wait_send()
            ecopy(c, d).wait_recv()


def entering(queries, keys, values, nz):
    tokens, width = keys.shape
    blocks = tokens // BLOCK
    nx, ng = lax.axis_size("seq") // nz, lax.axis_size("grp")
    rows = HEAD // nz
    hbm = pl.BlockSpec(memory_space=pltpu.HBM)
    vmem = pl.BlockSpec(memory_space=pltpu.VMEM)
    dma = pltpu.SemaphoreType.DMA
    outs = (
        pltpu.VMEM((CHANS, nz, rows, HEAD), F32),
        pltpu.VMEM((blocks, CHANS * HEAD, HEAD), F32),
        pltpu.VMEM((tokens, width), F32),
        pltpu.VMEM((tokens, width), F32),
        pltpu.VMEM((blocks, HEADS, BLOCK, BLOCK), F32),
        pltpu.VMEM((2, blocks, HEADS, HEAD, BLOCK), BF16),
        pltpu.VMEM((2, blocks, HEADS, BLOCK, HEAD), BF16),
        pltpu.VMEM((2, blocks, HEADS, BLOCK, HEAD), BF16),
    )
    e, loc, *rest = pl.pallas_call(
        functools.partial(scan_kernel, nz),
        out_shape=outs,
        in_specs=[hbm] * 3,
        out_specs=(vmem,) * len(outs),
        scratch_shapes=[
            pltpu.VMEM((tokens, width), F32),
            pltpu.VMEM((tokens, width), F32),
            pltpu.VMEM((CHANS, nz, rows, HEAD), F32),
            pltpu.VMEM((CHANS, nz, rows, HEAD), F32),
            pltpu.VMEM((CHANS, nz, rows, HEAD), F32),
            pltpu.VMEM((CHANS, nx, rows, HEAD), F32),
            pltpu.VMEM((CHANS, ng, rows, HEAD), F32),
            pltpu.VMEM((CHANS, nz, rows, HEAD), F32),
            dma, dma((HEADS, blocks)), dma((HEADS, blocks)),
            dma((CHANS, nz)), dma((CHANS, nz)), dma((CHANS, nx)), dma((CHANS, nx)),
            dma((CHANS, ng)), dma((CHANS, ng)), dma((CHANS, nz)), dma((CHANS, nz)),
        ],
        compiler_params=pltpu.CompilerParams(collective_id=0, has_side_effects=True, vmem_limit_bytes=57_500_000),
        name="scan",
    )(queries, keys, values)
    return e.reshape(CHANS * HEAD, HEAD), loc, *rest


def solve_kernel(e_ref, loc_ref, q_ref, img_ref, s_ref, kt_ref, kh_ref, vh_ref, out_ref):
    causal = causal_mask()

    def dots(a, b):
        return jnp.sum(a * b, axis=-1, keepdims=True)

    per = GROUP // BLOCK
    state = []
    for c in range(per):
        for h in range(HEADS):
            n = pl.program_id(0) * per + c
            row = pl.ds(pl.multiple_of(n * BLOCK, BLOCK), BLOCK)
            at = [pl.ds((2 * h + i) * HEAD, HEAD) for i in range(2)]
            enter = e_ref[at[0], :]
            q = q_ref[row, lanes(h)]
            state.append(dict(
                c=c, h=h, n=n, row=row, enter=halves(enter), gram=halves(enter + loc_ref[n, at[0], :]),
                state=halves(e_ref[at[1], :] + loc_ref[n, at[1], :]), x=None, r=q, p=q, rr=dots(q, q), acc=None))
    for step in range(ITERS):
        images, scores = [], []
        for st in state:
            n, h = st["n"], st["h"]
            p_hi, p_lo = halves(st["p"])
            if step == 0:
                scores.append(s_ref[n, h])
                images.append(narrow(p_hi, p_lo, *st["enter"]) + img_ref[st["row"], lanes(h)])
            else:
                sc = jnp.where(causal, scores_of(p_hi, p_lo, kt_ref[0, n, h], kt_ref[1, n, h]), 0.0)
                scores.append(sc)
                images.append(narrow(p_hi, p_lo, *st["gram"]) + weighted(sc, kh_ref[0, n, h], kh_ref[1, n, h]) + st["p"])
        for st, image, sc in zip(state, images, scores):
            alpha = st["rr"] / dots(st["p"], image)
            st["x"] = alpha * st["p"] if step == 0 else st["x"] + alpha * st["p"]
            st["acc"] = alpha * sc if step == 0 else st["acc"] + alpha * sc
            if step < ITERS - 1:
                st["r"] = st["r"] - alpha * image
                new = dots(st["r"], st["r"])
                st["p"] = st["r"] + new / st["rr"] * st["p"]
                st["rr"] = new
    first = lax.axis_index("grp") * lax.axis_size("seq") + lax.axis_index("seq")
    first = (first * pl.num_programs(0) + pl.program_id(0)) * GROUP
    for st in state:
        n, h = st["n"], st["h"]
        place = (first + st["c"] * BLOCK + lax.broadcasted_iota(jnp.int32, (BLOCK, HEAD), 0)).astype(F32)
        out = narrow(*halves(st["x"]), *st["state"]) + weighted(st["acc"], vh_ref[0, n, h], vh_ref[1, n, h])
        out_ref[pl.ds(st["c"] * BLOCK, BLOCK), lanes(h)] = out * jnp.sqrt(place + 1.0)


def solve(*parts):
    tokens, width = parts[2].shape
    return pl.pallas_call(
        solve_kernel,
        grid=(tokens // GROUP,),
        out_shape=jax.ShapeDtypeStruct((tokens, width), F32),
        in_specs=[pl.BlockSpec(memory_space=pltpu.VMEM)] * len(parts),
        out_specs=pl.BlockSpec((GROUP, width), lambda n: (n, 0)),
        compiler_params=pltpu.CompilerParams(vmem_limit_bytes=24 * 2**20),
        name="solve",
    )(*parts)


def on_device(queries, keys, values):
    return solve(*entering(queries, keys, values, ZDIM))


def solution(mesh):
    return jax.shard_map(
        on_device,
        mesh=mesh,
        in_specs=(P(("grp", "seq"), None), P(("grp", "seq"), None), P(("grp", "seq"), None)),
        out_specs=P(("grp", "seq"), None),
        check_vma=False,
    )
```

```python
import functools

import jax
import jax.numpy as jnp
from jax import lax
from jax.experimental import pallas as pl
from jax.experimental.pallas import tpu as pltpu
from jax.sharding import PartitionSpec as P

HEADS = 2
HEAD = 128
BLOCK = 256
ITERS = 4
ZDIM = 8
GROUP = 512
AHEAD = 3
F32 = jnp.float32
BF16 = jnp.bfloat16
MESH = pl.DeviceIdType.MESH


def halves(x):
    hi = x.astype(BF16)
    return hi, (x - hi.astype(F32)).astype(BF16)


def cat(*xs, axis):
    return jnp.concatenate(xs, axis=axis)


def mm(a, b):
    return jnp.dot(a, b, preferred_element_type=F32)


def mmt(a, b):
    return lax.dot_general(a, b, (((0,), (0,)), ((), ())), preferred_element_type=F32)


def narrow(a_hi, a_lo, b_hi, b_lo):
    right = cat(cat(b_hi, b_lo, axis=1), cat(b_hi, jnp.zeros_like(b_lo), axis=1), axis=0)
    t = mm(cat(a_hi, a_lo, axis=1), right)
    return t[:, :HEAD] + t[:, HEAD:]


def scores_of(a_hi, a_lo, kt_hi, kt_lo):
    return mm(cat(a_hi, a_lo, axis=1), cat(kt_hi, kt_hi, axis=0)) + mm(a_hi, kt_lo)


def weighted(s, b_hi, b_lo):
    s_hi, s_lo = halves(s)
    t = mm(s_hi, cat(b_hi, b_lo, axis=1))
    return t[:, :HEAD] + t[:, HEAD:] + mm(s_lo, b_hi)


def causal_mask():
    rows = lax.broadcasted_iota(jnp.int32, (BLOCK, BLOCK), 0)
    cols = lax.broadcasted_iota(jnp.int32, (BLOCK, BLOCK), 1)
    return cols <= rows


def lanes(h):
    return pl.ds(h * HEAD, HEAD)


def dots(a, b):
    return jnp.sum(a * b, axis=-1, keepdims=True)


def main_kernel(
    nz, q_hbm, k_hbm, v_hbm, x_ref, s_ref, vh_ref, state_ref,
    qbuf, kbuf, vbuf, img, kt, kh, near_a, near_b, near_s,
    sums, zin, zpre, xin, gin, eout, e,
    qsem, ksem, vsem, zs, zr, xs, xr, gs, gr, es, er,
):
    g, s = lax.axis_index("grp"), lax.axis_index("seq")
    ng, nx = lax.axis_size("grp"), lax.axis_size("seq") // nz
    z, x = s % nz, s // nz
    blocks = kbuf.shape[0] // BLOCK
    rows = HEADS * HEAD // nz

    def along_z(d):
        return {"grp": g, "seq": x * nz + (z + d) % nz}

    def along_x(d):
        return {"grp": g, "seq": ((x + d) % nx) * nz + z}

    def along_g(d):
        return {"grp": (g + d) % ng, "seq": s}

    def span(b):
        return pl.ds(b * BLOCK, BLOCK)

    k_loads = [pltpu.make_async_copy(k_hbm.at[span(b)], kbuf.at[span(b)], ksem.at[b]) for b in range(blocks)]
    v_loads = [pltpu.make_async_copy(v_hbm.at[span(b)], vbuf.at[span(b)], vsem.at[b]) for b in range(blocks)]
    q_load = pltpu.make_async_copy(q_hbm, qbuf, qsem)
    for load in k_loads + v_loads + [q_load]:
        load.start()
    barrier = pltpu.get_barrier_semaphore()
    partners = [along_z(d) for d in range(1, nz)] + [along_x(d) for d in range(1, nx)] + [along_g(d) for d in range(1, ng)]
    for partner in partners:
        pl.semaphore_signal(barrier, inc=1, device_id=partner, device_id_type=MESH)

    def remote(src, dst, send, recv, to):
        return pltpu.make_async_remote_copy(
            src_ref=src, dst_ref=dst, send_sem=send, recv_sem=recv, device_id=to, device_id_type=MESH)

    def zcopy(c, d):
        return remote(sums.at[c, (z + d) % nz], zin.at[c, z], zs.at[c, d], zr.at[c, d], along_z(d))

    def xcopy(c, d):
        return remote(xin.at[c, x], xin.at[c, x], xs.at[c, d], xr.at[c, d], along_x(d))

    def gcopy(c, d):
        return remote(gin.at[c, g], gin.at[c, g], gs.at[c, d], gr.at[c, d], along_g(d))

    def ecopy(c, d):
        return remote(eout.at[c, (z + d) % nz], e.at[c, z], es.at[c, d], er.at[c, d], along_z(d))

    far_first = sorted(range(1, nz), key=lambda d: -min(d, nz - d))
    half = nz // HEADS

    def send_sums(c, parts):
        for h, part in enumerate(parts):
            sums[c, pl.ds(h * half, half)] = part.reshape(half, rows, HEAD)
        for d in far_first:
            zcopy(c, d).start()
        zin[c, z] = sums[c, z]

    total_a = [jnp.zeros((HEAD, HEAD), F32) for _ in range(HEADS)]
    total_b = [jnp.zeros((HEAD, HEAD), F32) for _ in range(HEADS)]
    for b in range(blocks):
        k_loads[b].wait()
        for h in range(HEADS):
            k_hi, k_lo = halves(kbuf[span(b), lanes(h)])
            kh[0, b, h] = k_hi
            kh[1, b, h] = k_lo
            wide = mmt(k_hi, cat(k_hi, k_lo, axis=1))
            near_a[b, h] = total_a[h]
            near_b[b, h] = total_b[h]
            total_a[h] = total_a[h] + (wide[:, :HEAD] + wide[:, HEAD:])
            total_b[h] = total_b[h] + wide[:, HEAD:]
    grams = [total_a[h] + total_b[h].T for h in range(HEADS)]
    pl.semaphore_wait(barrier, len(partners))
    send_sums(0, grams)

    total_s = [jnp.zeros((HEAD, HEAD), F32) for _ in range(HEADS)]
    for b in range(blocks):
        v_loads[b].wait()
        for h in range(HEADS):
            v_hi, v_lo = halves(vbuf[span(b), lanes(h)])
            vh_ref[0, b, h] = v_hi
            vh_ref[1, b, h] = v_lo
            wide = mmt(kh[0, b, h], cat(v_hi, v_lo, axis=1))
            near_s[b, h] = total_s[h]
            total_s[h] = total_s[h] + (wide[:, :HEAD] + wide[:, HEAD:] + mmt(kh[1, b, h], v_hi))
    send_sums(1, total_s)

    q_load.wait()

    def local_part(b):
        causal = causal_mask()
        row = pl.ds(pl.multiple_of(b * BLOCK, BLOCK), BLOCK)
        for h in range(HEADS):
            q = qbuf[row, lanes(h)]
            q_hi, q_lo = halves(q)
            kt_hi, kt_lo = halves(kbuf[row, lanes(h)].T)
            kt[0, b, h] = kt_hi
            kt[1, b, h] = kt_lo
            scores = jnp.where(causal, scores_of(q_hi, q_lo, kt_hi, kt_lo), 0.0)
            s_ref[b, h] = scores
            gram = near_a[b, h] + near_b[b, h].T
            near_a[b, h] = gram
            near = weighted(scores, kh[0, b, h], kh[1, b, h])
            img[row, lanes(h)] = near + narrow(q_hi, q_lo, *halves(gram)) + q

    pl.loop(0, AHEAD)(local_part)

    zero = jnp.zeros((rows, HEAD), F32)
    held = {}

    def after_z(c):
        for d in range(1, nz):
            zcopy(c, d).wait_recv()
        run = zero
        for j in range(nz):
            zpre[c, j] = run
            run = run + zin[c, j]
        xin[c, x] = run
        for d in range(1, nx):
            xcopy(c, d).start()

    def after_x(c):
        for d in range(1, nx):
            xcopy(c, d).wait_recv()
        before, whole = zero, zero
        for j in range(nx):
            piece = xin[c, j]
            before = before + jnp.where(j < x, piece, 0.0)
            whole = whole + piece
        held[c] = before
        gin[c, g] = whole
        for d in range(1, ng):
            @pl.when(g + d < ng)
            def _():
                gcopy(c, d).start()

    def after_g(c):
        for d in range(1, ng):
            @pl.when(g - d >= 0)
            def _():
                gcopy(c, d).wait_recv()
        before = held[c] + lax.fori_loop(0, g, lambda j, acc: acc + gin[c, j], zero)
        for j in range(nz):
            eout[c, j] = zpre[c, j] + before
        for d in far_first:
            ecopy(c, d).start()
        e[c, z] = eout[c, z]

    for c in range(2):
        after_z(c)
    for c in range(2):
        after_x(c)
    for c in range(2):
        after_g(c)
    pl.loop(AHEAD, blocks)(local_part)
    for d in range(1, nz):
        ecopy(0, d).wait_recv()

    @pl.loop(0, blocks * BLOCK // GROUP)
    def _(i):
        causal = causal_mask()
        work = []
        for c in range(GROUP // BLOCK):
            for h in range(HEADS):
                n = i * (GROUP // BLOCK) + c
                row = pl.ds(pl.multiple_of(n * BLOCK, BLOCK), BLOCK)
                enter = e[0, pl.ds(h * half, half)].reshape(HEAD, HEAD)
                q = qbuf[row, lanes(h)]
                work.append(dict(
                    n=n, h=h, row=row, enter=halves(enter), gram=halves(enter + near_a[n, h]),
                    x=None, r=q, p=q, rr=dots(q, q), acc=None))
        for step in range(ITERS):
            images, scores = [], []
            for st in work:
                n, h = st["n"], st["h"]
                p_hi, p_lo = halves(st["p"])
                if step == 0:
                    scores.append(s_ref[n, h])
                    images.append(narrow(p_hi, p_lo, *st["enter"]) + img[st["row"], lanes(h)])
                else:
                    sc = jnp.where(causal, scores_of(p_hi, p_lo, kt[0, n, h], kt[1, n, h]), 0.0)
                    scores.append(sc)
                    images.append(narrow(p_hi, p_lo, *st["gram"]) + weighted(sc, kh[0, n, h], kh[1, n, h]) + st["p"])
            for st, image, sc in zip(work, images, scores):
                alpha = st["rr"] / dots(st["p"], image)
                st["x"] = alpha * st["p"] if step == 0 else st["x"] + alpha * st["p"]
                st["acc"] = alpha * sc if step == 0 else st["acc"] + alpha * sc
                if step < ITERS - 1:
                    st["r"] = st["r"] - alpha * image
                    new = dots(st["r"], st["r"])
                    st["p"] = st["r"] + new / st["rr"] * st["p"]
                    st["rr"] = new
        for st in work:
            x_ref[st["row"], lanes(st["h"])] = st["x"]
            s_ref[st["n"], st["h"]] = st["acc"]

    for d in range(1, nz):
        ecopy(1, d).wait_recv()
    for h in range(HEADS):
        for b in range(blocks):
            hi, lo = halves(e[1, pl.ds(h * half, half)].reshape(HEAD, HEAD) + near_s[b, h])
            state_ref[0, b, h] = hi
            state_ref[1, b, h] = lo
    for c in range(2):
        for d in range(1, nz):
            zcopy(c, d).wait_send()
            ecopy(c, d).wait_send()
        for d in range(1, nx):
            xcopy(c, d).wait_send()
        for d in range(1, ng):
            @pl.when(g + d < ng)
            def _():
                gcopy(c, d).wait_send()


def steps(queries, keys, values, nz):
    tokens, width = keys.shape
    blocks = tokens // BLOCK
    nx, ng = lax.axis_size("seq") // nz, lax.axis_size("grp")
    rows = HEADS * HEAD // nz
    hbm = pl.BlockSpec(memory_space=pltpu.HBM)
    vmem = pl.BlockSpec(memory_space=pltpu.VMEM)
    dma = pltpu.SemaphoreType.DMA
    outs = (
        pltpu.VMEM((tokens, width), F32),
        pltpu.VMEM((blocks, HEADS, BLOCK, BLOCK), F32),
        pltpu.VMEM((2, blocks, HEADS, BLOCK, HEAD), BF16),
        pltpu.VMEM((2, blocks, HEADS, HEAD, HEAD), BF16),
    )
    square = pltpu.VMEM((blocks, HEADS, HEAD, HEAD), F32)
    pieces = pltpu.VMEM((2, nz, rows, HEAD), F32)
    return pl.pallas_call(
        functools.partial(main_kernel, nz),
        out_shape=outs,
        in_specs=[hbm] * 3,
        out_specs=(vmem,) * len(outs),
        scratch_shapes=[
            pltpu.VMEM((tokens, width), F32),
            pltpu.VMEM((tokens, width), F32),
            pltpu.VMEM((tokens, width), F32),
            pltpu.VMEM((tokens, width), F32),
            pltpu.VMEM((2, blocks, HEADS, HEAD, BLOCK), BF16),
            pltpu.VMEM((2, blocks, HEADS, BLOCK, HEAD), BF16),
            square, square, square,
            pieces, pieces, pieces,
            pltpu.VMEM((2, nx, rows, HEAD), F32),
            pltpu.VMEM((2, ng, rows, HEAD), F32),
            pieces, pieces,
            dma, dma((blocks,)), dma((blocks,)),
            dma((2, nz)), dma((2, nz)), dma((2, nx)), dma((2, nx)),
            dma((2, ng)), dma((2, ng)), dma((2, nz)), dma((2, nz)),
        ],
        compiler_params=pltpu.CompilerParams(collective_id=0, has_side_effects=True, vmem_limit_bytes=61_600_000),
        name="steps",
    )(queries, keys, values)


def last_kernel(x_ref, s_ref, vh_ref, state_ref, out_ref):
    first = lax.axis_index("grp") * lax.axis_size("seq") + lax.axis_index("seq")
    first = (first * pl.num_programs(0) + pl.program_id(0)) * BLOCK
    scale = jnp.sqrt((first + lax.broadcasted_iota(jnp.int32, (BLOCK, HEAD), 0)).astype(F32) + 1.0)
    n = pl.program_id(0)
    row = pl.ds(pl.multiple_of(n * BLOCK, BLOCK), BLOCK)
    for h in range(HEADS):
        out = narrow(*halves(x_ref[row, lanes(h)]), state_ref[0, n, h], state_ref[1, n, h])
        out = out + weighted(s_ref[n, h], vh_ref[0, n, h], vh_ref[1, n, h])
        out_ref[:, lanes(h)] = out * scale


def last(*parts):
    tokens, width = parts[0].shape
    return pl.pallas_call(
        last_kernel,
        grid=(tokens // BLOCK,),
        out_shape=jax.ShapeDtypeStruct((tokens, width), F32),
        in_specs=[pl.BlockSpec(memory_space=pltpu.VMEM)] * len(parts),
        out_specs=pl.BlockSpec((BLOCK, width), lambda n: (n, 0)),
        compiler_params=pltpu.CompilerParams(vmem_limit_bytes=16 * 2**20),
        name="last",
    )(*parts)


def on_device(queries, keys, values):
    return last(*steps(queries, keys, values, ZDIM))


def solution(mesh):
    return jax.shard_map(
        on_device,
        mesh=mesh,
        in_specs=(P(("grp", "seq"), None), P(("grp", "seq"), None), P(("grp", "seq"), None)),
        out_specs=P(("grp", "seq"), None),
        check_vma=False,
    )
```

```python
import functools

import jax
import jax.numpy as jnp
from jax import lax
from jax.experimental import pallas as pl
from jax.experimental.pallas import tpu as pltpu
from jax.sharding import PartitionSpec as P

HEADS = 2
HEAD = 128
BLOCK = 256
ITERS = 4
ZDIM = 8
GROUP = 1024
AHEAD = 3
F32 = jnp.float32
BF16 = jnp.bfloat16
MESH = pl.DeviceIdType.MESH


def halves(x):
    hi = x.astype(BF16)
    return hi, (x - hi.astype(F32)).astype(BF16)


def cat(*xs, axis):
    return jnp.concatenate(xs, axis=axis)


def mm(a, b):
    return jnp.dot(a, b, preferred_element_type=F32)


def mmt(a, b):
    return lax.dot_general(a, b, (((0,), (0,)), ((), ())), preferred_element_type=F32)


def narrow(a_hi, a_lo, b_hi, b_lo):
    right = cat(cat(b_hi, b_lo, axis=1), cat(b_hi, jnp.zeros_like(b_lo), axis=1), axis=0)
    t = mm(cat(a_hi, a_lo, axis=1), right)
    return t[:, :HEAD] + t[:, HEAD:]


def scores_of(a_hi, a_lo, kt_hi, kt_lo):
    t = mm(cat(a_hi, a_lo, axis=0), kt_hi)
    return t[:BLOCK] + t[BLOCK:] + mm(a_hi, kt_lo)


def weighted(s, b_hi, b_lo):
    s_hi, s_lo = halves(s)
    t = mm(cat(s_hi, s_lo, axis=0), cat(b_hi, b_lo, axis=1))
    return t[:BLOCK, :HEAD] + t[:BLOCK, HEAD:] + t[BLOCK:, :HEAD]


def causal_mask():
    rows = lax.broadcasted_iota(jnp.int32, (BLOCK, BLOCK), 0)
    cols = lax.broadcasted_iota(jnp.int32, (BLOCK, BLOCK), 1)
    return cols <= rows


def lanes(h):
    return pl.ds(h * HEAD, HEAD)


def dots(a, b):
    return jnp.sum(a * b, axis=-1, keepdims=True)


def main_kernel(
    nz, q_hbm, k_hbm, v_hbm, x_ref, near_ref, state_ref,
    qbuf, kbuf, vbuf, img, s_ref, kt, kh, vh, near_a, near_b, near_s,
    sums, zin, zpre, xin, gin, eout, e,
    qsem, ksem, vsem, zs, zr, xs, xr, gs, gr, es, er,
):
    g, s = lax.axis_index("grp"), lax.axis_index("seq")
    ng, nx = lax.axis_size("grp"), lax.axis_size("seq") // nz
    z, x = s % nz, s // nz
    blocks = kbuf.shape[0] // BLOCK
    rows = HEADS * HEAD // nz

    def along_z(d):
        return {"grp": g, "seq": x * nz + (z + d) % nz}

    def along_x(d):
        return {"grp": g, "seq": ((x + d) % nx) * nz + z}

    def along_g(d):
        return {"grp": (g + d) % ng, "seq": s}

    def span(b):
        return pl.ds(b * BLOCK, BLOCK)

    k_loads = [pltpu.make_async_copy(k_hbm.at[span(b)], kbuf.at[span(b)], ksem.at[b]) for b in range(blocks)]
    v_loads = [pltpu.make_async_copy(v_hbm.at[span(b)], vbuf.at[span(b)], vsem.at[b]) for b in range(blocks)]
    q_load = pltpu.make_async_copy(q_hbm, qbuf, qsem)
    for load in k_loads:
        load.start()
    barrier = pltpu.get_barrier_semaphore()
    partners = [along_z(d) for d in range(1, nz)] + [along_x(d) for d in range(1, nx)] + [along_g(d) for d in range(1, ng)]
    for partner in partners:
        pl.semaphore_signal(barrier, inc=1, device_id=partner, device_id_type=MESH)

    def remote(src, dst, send, recv, to):
        return pltpu.make_async_remote_copy(
            src_ref=src, dst_ref=dst, send_sem=send, recv_sem=recv, device_id=to, device_id_type=MESH)

    def zcopy(c, d):
        return remote(sums.at[c, (z + d) % nz], zin.at[c, z], zs.at[c, d], zr.at[c, d], along_z(d))

    def xcopy(c, d):
        return remote(xin.at[c, x], xin.at[c, x], xs.at[c, d], xr.at[c, d], along_x(d))

    def gcopy(c, d):
        return remote(gin.at[c, g], gin.at[c, g], gs.at[c, d], gr.at[c, d], along_g(d))

    def ecopy(c, d):
        return remote(eout.at[c, (z + d) % nz], e.at[c, z], es.at[c, d], er.at[c, d], along_z(d))

    far_first = sorted(range(1, nz), key=lambda d: -min(d, nz - d))
    half = nz // HEADS

    def keep_sums(c, parts):
        for h, part in enumerate(parts):
            sums[c, pl.ds(h * half, half)] = part.reshape(half, rows, HEAD)

    def send_sums(c):
        for d in far_first:
            zcopy(c, d).start()
        zin[c, z] = sums[c, z]

    total_a = [jnp.zeros((HEAD, HEAD), F32) for _ in range(HEADS)]
    total_b = [jnp.zeros((HEAD, HEAD), F32) for _ in range(HEADS)]
    for b in range(blocks):
        k_loads[b].wait()
        if b == blocks - 1:
            for load in v_loads + [q_load]:
                load.start()
        for h in range(HEADS):
            k_hi, k_lo = halves(kbuf[span(b), lanes(h)])
            kh[0, b, h] = k_hi
            kh[1, b, h] = k_lo
            wide = mmt(k_hi, cat(k_hi, k_lo, axis=1))
            near_a[b, h] = total_a[h]
            near_b[b, h] = total_b[h]
            total_a[h] = total_a[h] + (wide[:, :HEAD] + wide[:, HEAD:])
            total_b[h] = total_b[h] + wide[:, HEAD:]
    grams = [total_a[h] + total_b[h].T for h in range(HEADS)]
    pl.semaphore_wait(barrier, len(partners))
    keep_sums(0, grams)
    send_sums(0)

    total_s = [jnp.zeros((HEAD, HEAD), F32) for _ in range(HEADS)]
    for b in range(blocks):
        v_loads[b].wait()
        for h in range(HEADS):
            v_hi, v_lo = halves(vbuf[span(b), lanes(h)])
            vh[0, b, h] = v_hi
            vh[1, b, h] = v_lo
            wide = mmt(kh[0, b, h], cat(v_hi, v_lo, axis=1))
            near_s[b, h] = total_s[h]
            total_s[h] = total_s[h] + (wide[:, :HEAD] + wide[:, HEAD:] + mmt(kh[1, b, h], v_hi))
    keep_sums(1, total_s)

    q_load.wait()

    def local_part(b):
        causal = causal_mask()
        row = pl.ds(pl.multiple_of(b * BLOCK, BLOCK), BLOCK)
        for h in range(HEADS):
            q = qbuf[row, lanes(h)]
            q_hi, q_lo = halves(q)
            kt_hi, kt_lo = halves(kbuf[row, lanes(h)].T)
            kt[0, b, h] = kt_hi
            kt[1, b, h] = kt_lo
            scores = jnp.where(causal, scores_of(q_hi, q_lo, kt_hi, kt_lo), 0.0)
            s_ref[b, h] = scores
            gram = near_a[b, h] + near_b[b, h].T
            near_a[b, h] = gram
            near = weighted(scores, kh[0, b, h], kh[1, b, h])
            img[row, lanes(h)] = near + narrow(q_hi, q_lo, *halves(gram)) + q

    pl.loop(0, AHEAD)(local_part)

    zero = jnp.zeros((rows, HEAD), F32)
    held = {}

    def after_z(c):
        for d in range(1, nz):
            zcopy(c, d).wait_recv()
        run = zero
        for j in range(nz):
            zpre[c, j] = run
            run = run + zin[c, j]
        xin[c, x] = run
        for d in range(1, nx):
            xcopy(c, d).start()

    def after_x(c):
        for d in range(1, nx):
            xcopy(c, d).wait_recv()
        before, whole = zero, zero
        for j in range(nx):
            piece = xin[c, j]
            before = before + jnp.where(j < x, piece, 0.0)
            whole = whole + piece
        held[c] = before
        gin[c, g] = whole
        for d in range(1, ng):
            @pl.when(g + d < ng)
            def _():
                gcopy(c, d).start()

    def after_g(c):
        for d in range(1, ng):
            @pl.when(g - d >= 0)
            def _():
                gcopy(c, d).wait_recv()
        before = held[c] + lax.fori_loop(0, g, lambda j, acc: acc + gin[c, j], zero)
        for j in range(nz):
            eout[c, j] = zpre[c, j] + before
        for d in far_first:
            ecopy(c, d).start()
        e[c, z] = eout[c, z]

    def solve_group(i):
        causal = causal_mask()
        work = []
        for c in range(GROUP // BLOCK):
            for h in range(HEADS):
                n = i * (GROUP // BLOCK) + c
                row = pl.ds(pl.multiple_of(n * BLOCK, BLOCK), BLOCK)
                enter = e[0, pl.ds(h * half, half)].reshape(HEAD, HEAD)
                q = qbuf[row, lanes(h)]
                work.append(dict(
                    n=n, h=h, row=row, enter=halves(enter), gram=halves(enter + near_a[n, h]),
                    x=None, r=q, p=q, rr=dots(q, q), acc=None))
        for step in range(ITERS):
            images, scores = [], []
            for st in work:
                n, h = st["n"], st["h"]
                p_hi, p_lo = halves(st["p"])
                if step == 0:
                    scores.append(s_ref[n, h])
                    images.append(narrow(p_hi, p_lo, *st["enter"]) + img[st["row"], lanes(h)])
                else:
                    sc = jnp.where(causal, scores_of(p_hi, p_lo, kt[0, n, h], kt[1, n, h]), 0.0)
                    scores.append(sc)
                    images.append(narrow(p_hi, p_lo, *st["gram"]) + weighted(sc, kh[0, n, h], kh[1, n, h]) + st["p"])
            for st, image, sc in zip(work, images, scores):
                alpha = st["rr"] / dots(st["p"], image)
                st["x"] = alpha * st["p"] if step == 0 else st["x"] + alpha * st["p"]
                st["acc"] = alpha * sc if step == 0 else st["acc"] + alpha * sc
                if step < ITERS - 1:
                    st["r"] = st["r"] - alpha * image
                    new = dots(st["r"], st["r"])
                    st["p"] = st["r"] + new / st["rr"] * st["p"]
                    st["rr"] = new
        for st in work:
            n, h = st["n"], st["h"]
            x_ref[st["row"], lanes(h)] = st["x"]
            near_ref[st["row"], lanes(h)] = weighted(st["acc"], vh[0, n, h], vh[1, n, h])

    groups = blocks * BLOCK // GROUP
    after_z(0)
    send_sums(1)
    after_x(0)
    after_z(1)
    after_g(0)
    after_x(1)
    pl.loop(AHEAD, blocks)(local_part)
    after_g(1)
    for d in range(1, nz):
        ecopy(0, d).wait_recv()
    pl.loop(0, groups)(solve_group)
    for d in range(1, nz):
        ecopy(1, d).wait_recv()
    for h in range(HEADS):
        for b in range(blocks):
            hi, lo = halves(e[1, pl.ds(h * half, half)].reshape(HEAD, HEAD) + near_s[b, h])
            state_ref[0, b, h] = hi
            state_ref[1, b, h] = lo
    for c in range(2):
        for d in range(1, nz):
            zcopy(c, d).wait_send()
            ecopy(c, d).wait_send()
        for d in range(1, nx):
            xcopy(c, d).wait_send()
        for d in range(1, ng):
            @pl.when(g + d < ng)
            def _():
                gcopy(c, d).wait_send()


def steps(queries, keys, values, nz):
    tokens, width = keys.shape
    blocks = tokens // BLOCK
    nx, ng = lax.axis_size("seq") // nz, lax.axis_size("grp")
    rows = HEADS * HEAD // nz
    hbm = pl.BlockSpec(memory_space=pltpu.HBM)
    vmem = pl.BlockSpec(memory_space=pltpu.VMEM)
    dma = pltpu.SemaphoreType.DMA
    outs = (
        pltpu.VMEM((tokens, width), F32),
        pltpu.VMEM((tokens, width), F32),
        pltpu.VMEM((2, blocks, HEADS, HEAD, HEAD), BF16),
    )
    square = pltpu.VMEM((blocks, HEADS, HEAD, HEAD), F32)
    pieces = pltpu.VMEM((2, nz, rows, HEAD), F32)
    return pl.pallas_call(
        functools.partial(main_kernel, nz),
        out_shape=outs,
        in_specs=[hbm] * 3,
        out_specs=(vmem,) * len(outs),
        scratch_shapes=[
            pltpu.VMEM((tokens, width), F32),
            pltpu.VMEM((tokens, width), F32),
            pltpu.VMEM((tokens, width), F32),
            pltpu.VMEM((tokens, width), F32),
            pltpu.VMEM((blocks, HEADS, BLOCK, BLOCK), F32),
            pltpu.VMEM((2, blocks, HEADS, HEAD, BLOCK), BF16),
            pltpu.VMEM((2, blocks, HEADS, BLOCK, HEAD), BF16),
            pltpu.VMEM((2, blocks, HEADS, BLOCK, HEAD), BF16),
            square, square, square,
            pieces, pieces, pieces,
            pltpu.VMEM((2, nx, rows, HEAD), F32),
            pltpu.VMEM((2, ng, rows, HEAD), F32),
            pieces, pieces,
            dma, dma((blocks,)), dma((blocks,)),
            dma((2, nz)), dma((2, nz)), dma((2, nx)), dma((2, nx)),
            dma((2, ng)), dma((2, ng)), dma((2, nz)), dma((2, nz)),
        ],
        compiler_params=pltpu.CompilerParams(collective_id=0, has_side_effects=True, vmem_limit_bytes=63_400_000),
        name="steps",
    )(queries, keys, values)


def last_kernel(x_ref, near_ref, state_ref, out_ref):
    first = lax.axis_index("grp") * lax.axis_size("seq") + lax.axis_index("seq")
    first = (first * pl.num_programs(0) + pl.program_id(0)) * GROUP
    for c in range(GROUP // BLOCK):
        n = pl.program_id(0) * (GROUP // BLOCK) + c
        row = pl.ds(pl.multiple_of(n * BLOCK, BLOCK), BLOCK)
        place = (first + c * BLOCK + lax.broadcasted_iota(jnp.int32, (BLOCK, HEAD), 0)).astype(F32)
        scale = jnp.sqrt(place + 1.0)
        for h in range(HEADS):
            out = narrow(*halves(x_ref[row, lanes(h)]), state_ref[0, n, h], state_ref[1, n, h])
            out_ref[pl.ds(c * BLOCK, BLOCK), lanes(h)] = (out + near_ref[row, lanes(h)]) * scale


def last(*parts):
    tokens, width = parts[0].shape
    return pl.pallas_call(
        last_kernel,
        grid=(tokens // GROUP,),
        out_shape=jax.ShapeDtypeStruct((tokens, width), F32),
        in_specs=[pl.BlockSpec(memory_space=pltpu.VMEM)] * len(parts),
        out_specs=pl.BlockSpec((GROUP, width), lambda n: (n, 0)),
        compiler_params=pltpu.CompilerParams(vmem_limit_bytes=16 * 2**20),
        name="last",
    )(*parts)


def on_device(queries, keys, values):
    return last(*steps(queries, keys, values, ZDIM))


def solution(mesh):
    return jax.shard_map(
        on_device,
        mesh=mesh,
        in_specs=(P(("grp", "seq"), None), P(("grp", "seq"), None), P(("grp", "seq"), None)),
        out_specs=P(("grp", "seq"), None),
        check_vma=False,
    )
```

```python
import functools

import jax
import jax.numpy as jnp
from jax import lax
from jax.experimental import pallas as pl
from jax.experimental.pallas import tpu as pltpu
from jax.sharding import PartitionSpec as P

HEADS = 2
HEAD = 128
BLOCK = 256
ITERS = 4
ZDIM = 8
GROUP = 1024
AHEAD = 3
F32 = jnp.float32
BF16 = jnp.bfloat16
MESH = pl.DeviceIdType.MESH


def halves(x):
    hi = x.astype(BF16)
    return hi, (x - hi.astype(F32)).astype(BF16)


def cat(*xs, axis):
    return jnp.concatenate(xs, axis=axis)


def mm(a, b):
    return jnp.dot(a, b, preferred_element_type=F32)


def mmt(a, b):
    return lax.dot_general(a, b, (((0,), (0,)), ((), ())), preferred_element_type=F32)


def narrow(a_hi, a_lo, b_hi, b_lo):
    right = cat(cat(b_hi, b_lo, axis=1), cat(b_hi, jnp.zeros_like(b_lo), axis=1), axis=0)
    t = mm(cat(a_hi, a_lo, axis=1), right)
    return t[:, :HEAD] + t[:, HEAD:]


def scores_of(a_hi, a_lo, kt_hi, kt_lo):
    t = mm(cat(a_hi, a_lo, axis=0), kt_hi)
    return t[:BLOCK] + t[BLOCK:] + mm(a_hi, kt_lo)


def weighted(s, b_hi, b_lo):
    s_hi, s_lo = halves(s)
    t = mm(cat(s_hi, s_lo, axis=0), cat(b_hi, b_lo, axis=1))
    return t[:BLOCK, :HEAD] + t[:BLOCK, HEAD:] + t[BLOCK:, :HEAD]


def causal_mask():
    rows = lax.broadcasted_iota(jnp.int32, (BLOCK, BLOCK), 0)
    cols = lax.broadcasted_iota(jnp.int32, (BLOCK, BLOCK), 1)
    return cols <= rows


def lanes(h):
    return pl.ds(h * HEAD, HEAD)


def dots(a, b):
    return jnp.sum(a * b, axis=-1, keepdims=True)


def energy(a, b):
    return jnp.sum(a + (b[:, :HEAD] + b[:, HEAD:]), axis=-1, keepdims=True)


def main_kernel(
    nz, q_hbm, k_hbm, v_hbm, x_ref, near_ref, state_ref,
    qbuf, kbuf, vbuf, img, s_ref, kt, kh, vh, near_a, near_b, near_s,
    sums, zin, zpre, xin, gin, eout, e,
    qsem, ksem, vsem, zs, zr, xs, xr, gs, gr, es, er,
):
    blocks = kbuf.shape[0] // BLOCK
    rows = HEADS * HEAD // nz

    def span(b):
        return pl.ds(b * BLOCK, BLOCK)

    k_loads = [pltpu.make_async_copy(k_hbm.at[span(b)], kbuf.at[span(b)], ksem.at[b]) for b in range(blocks)]
    v_loads = [pltpu.make_async_copy(v_hbm.at[span(b)], vbuf.at[span(b)], vsem.at[b]) for b in range(blocks)]
    q_load = pltpu.make_async_copy(q_hbm, qbuf, qsem)
    for load in k_loads:
        load.start()
    g, s = lax.axis_index("grp"), lax.axis_index("seq")
    ng, nx = lax.axis_size("grp"), lax.axis_size("seq") // nz
    z, x = s % nz, s // nz

    def along_z(d):
        return {"grp": g, "seq": x * nz + (z + d) % nz}

    def along_x(d):
        return {"grp": g, "seq": ((x + d) % nx) * nz + z}

    def along_g(d):
        return {"grp": (g + d) % ng, "seq": s}

    barrier = pltpu.get_barrier_semaphore()
    partners = [along_z(d) for d in range(1, nz)] + [along_x(d) for d in range(1, nx)] + [along_g(d) for d in range(1, ng)]
    for partner in partners:
        pl.semaphore_signal(barrier, inc=1, device_id=partner, device_id_type=MESH)

    def remote(src, dst, send, recv, to):
        return pltpu.make_async_remote_copy(
            src_ref=src, dst_ref=dst, send_sem=send, recv_sem=recv, device_id=to, device_id_type=MESH)

    def zcopy(c, d):
        return remote(sums.at[c, (z + d) % nz], zin.at[c, z], zs.at[c, d], zr.at[c, d], along_z(d))

    def xcopy(c, d):
        return remote(xin.at[c, x], xin.at[c, x], xs.at[c, d], xr.at[c, d], along_x(d))

    def gcopy(c, d):
        return remote(gin.at[c, g], gin.at[c, g], gs.at[c, d], gr.at[c, d], along_g(d))

    def ecopy(c, d):
        return remote(eout.at[c, (z + d) % nz], e.at[c, z], es.at[c, d], er.at[c, d], along_z(d))

    far_first = sorted(range(1, nz), key=lambda d: -min(d, nz - d))
    half = nz // HEADS

    def keep_sums(c, parts):
        for h, part in enumerate(parts):
            sums[c, pl.ds(h * half, half)] = part.reshape(half, rows, HEAD)

    def send_sums(c):
        for d in far_first:
            zcopy(c, d).start()
        zin[c, z] = sums[c, z]

    total_a = [jnp.zeros((HEAD, HEAD), F32) for _ in range(HEADS)]
    total_b = [jnp.zeros((HEAD, HEAD), F32) for _ in range(HEADS)]
    for b in range(blocks):
        k_loads[b].wait()
        if b == blocks - 1:
            for load in v_loads + [q_load]:
                load.start()
        for h in range(HEADS):
            k_hi, k_lo = halves(kbuf[span(b), lanes(h)])
            kh[0, b, h] = k_hi
            kh[1, b, h] = k_lo
            wide = mmt(k_hi, cat(k_hi, k_lo, axis=1))
            near_a[b, h] = total_a[h]
            near_b[b, h] = total_b[h]
            total_a[h] = total_a[h] + (wide[:, :HEAD] + wide[:, HEAD:])
            total_b[h] = total_b[h] + wide[:, HEAD:]
    grams = [total_a[h] + total_b[h].T for h in range(HEADS)]
    pl.semaphore_wait(barrier, len(partners))
    keep_sums(0, grams)
    send_sums(0)

    total_s = [jnp.zeros((HEAD, HEAD), F32) for _ in range(HEADS)]
    for b in range(blocks):
        v_loads[b].wait()
        for h in range(HEADS):
            v_hi, v_lo = halves(vbuf[span(b), lanes(h)])
            vh[0, b, h] = v_hi
            vh[1, b, h] = v_lo
            wide = mmt(kh[0, b, h], cat(v_hi, v_lo, axis=1))
            near_s[b, h] = total_s[h]
            total_s[h] = total_s[h] + (wide[:, :HEAD] + wide[:, HEAD:] + mmt(kh[1, b, h], v_hi))
    keep_sums(1, total_s)

    q_load.wait()

    def local_part(b):
        causal = causal_mask()
        row = pl.ds(pl.multiple_of(b * BLOCK, BLOCK), BLOCK)
        for h in range(HEADS):
            q = qbuf[row, lanes(h)]
            q_hi, q_lo = halves(q)
            kt_hi, kt_lo = halves(kbuf[row, lanes(h)].T)
            kt[0, b, h] = kt_hi
            kt[1, b, h] = kt_lo
            scores = jnp.where(causal, scores_of(q_hi, q_lo, kt_hi, kt_lo), 0.0)
            s_ref[b, h] = scores
            gram = near_a[b, h] + near_b[b, h].T
            near_a[b, h] = gram
            near = weighted(scores, kh[0, b, h], kh[1, b, h])
            img[row, lanes(h)] = near + narrow(q_hi, q_lo, *halves(gram)) + q

    pl.loop(0, AHEAD)(local_part)

    zero = jnp.zeros((rows, HEAD), F32)
    held = {}

    def after_z(c):
        for d in range(1, nz):
            zcopy(c, d).wait_recv()
        run = zero
        for j in range(nz):
            zpre[c, j] = run
            run = run + zin[c, j]
        xin[c, x] = run
        for d in range(1, nx):
            xcopy(c, d).start()

    def after_x(c):
        for d in range(1, nx):
            xcopy(c, d).wait_recv()
        before, whole = zero, zero
        for j in range(nx):
            piece = xin[c, j]
            before = before + jnp.where(j < x, piece, 0.0)
            whole = whole + piece
        held[c] = before
        gin[c, g] = whole
        for d in range(1, ng):
            @pl.when(g + d < ng)
            def _():
                gcopy(c, d).start()

    def after_g(c):
        for d in range(1, ng):
            @pl.when(g - d >= 0)
            def _():
                gcopy(c, d).wait_recv()
        before = held[c] + lax.fori_loop(0, g, lambda j, acc: acc + gin[c, j], zero)
        for j in range(nz):
            eout[c, j] = zpre[c, j] + before
        for i in range(nz - 1):
            ecopy(c, (i + (i >= z).astype(jnp.int32) - z + nz) % nz).start()
        e[c, z] = eout[c, z]

    def solve_group(i):
        causal = causal_mask()
        work = []
        for c in range(GROUP // BLOCK):
            for h in range(HEADS):
                n = i * (GROUP // BLOCK) + c
                row = pl.ds(pl.multiple_of(n * BLOCK, BLOCK), BLOCK)
                enter = e[0, pl.ds(h * half, half)].reshape(HEAD, HEAD)
                q = qbuf[row, lanes(h)]
                work.append(dict(
                    n=n, h=h, row=row, enter=halves(enter), gram=halves(enter + near_a[n, h]),
                    x=None, r=q, p=q, rr=dots(q, q), acc=None))
        for step in range(ITERS):
            images, scores = [], []
            for st in work:
                n, h = st["n"], st["h"]
                p_hi, p_lo = halves(st["p"])
                if step == 0:
                    scores.append(s_ref[n, h])
                    images.append(narrow(p_hi, p_lo, *st["enter"]) + img[st["row"], lanes(h)])
                else:
                    sc = jnp.where(causal, scores_of(p_hi, p_lo, kt[0, n, h], kt[1, n, h]), 0.0)
                    scores.append(sc)
                    image = narrow(p_hi, p_lo, *st["gram"]) + st["p"]
                    images.append(image if step == ITERS - 1 else image + weighted(sc, kh[0, n, h], kh[1, n, h]))
            for st, image, sc in zip(work, images, scores):
                if step == ITERS - 1:
                    alpha = st["rr"] / energy(st["p"] * image, sc * sc)
                else:
                    alpha = st["rr"] / dots(st["p"], image)
                st["x"] = alpha * st["p"] if step == 0 else st["x"] + alpha * st["p"]
                st["acc"] = alpha * sc if step == 0 else st["acc"] + alpha * sc
                if step < ITERS - 1:
                    st["r"] = st["r"] - alpha * image
                    new = dots(st["r"], st["r"])
                    st["p"] = st["r"] + new / st["rr"] * st["p"]
                    st["rr"] = new
        for st in work:
            n, h = st["n"], st["h"]
            x_ref[st["row"], lanes(h)] = st["x"]
            near_ref[st["row"], lanes(h)] = weighted(st["acc"], vh[0, n, h], vh[1, n, h])

    groups = blocks * BLOCK // GROUP
    after_z(0)
    send_sums(1)
    after_x(0)
    after_z(1)
    after_g(0)
    after_x(1)
    pl.loop(AHEAD, blocks)(local_part)
    after_g(1)
    for d in range(1, nz):
        ecopy(0, d).wait_recv()
    pl.loop(0, groups)(solve_group)
    for d in range(1, nz):
        ecopy(1, d).wait_recv()
    for h in range(HEADS):
        for b in range(blocks):
            hi, lo = halves(e[1, pl.ds(h * half, half)].reshape(HEAD, HEAD) + near_s[b, h])
            state_ref[0, b, h] = hi
            state_ref[1, b, h] = lo
    for c in range(2):
        for d in range(1, nz):
            zcopy(c, d).wait_send()
            ecopy(c, d).wait_send()
        for d in range(1, nx):
            xcopy(c, d).wait_send()
        for d in range(1, ng):
            @pl.when(g + d < ng)
            def _():
                gcopy(c, d).wait_send()


def steps(queries, keys, values, nz):
    tokens, width = keys.shape
    blocks = tokens // BLOCK
    nx, ng = lax.axis_size("seq") // nz, lax.axis_size("grp")
    rows = HEADS * HEAD // nz
    hbm = pl.BlockSpec(memory_space=pltpu.HBM)
    vmem = pl.BlockSpec(memory_space=pltpu.VMEM)
    dma = pltpu.SemaphoreType.DMA
    outs = (
        pltpu.VMEM((tokens, width), F32),
        pltpu.VMEM((tokens, width), F32),
        pltpu.VMEM((2, blocks, HEADS, HEAD, HEAD), BF16),
    )
    square = pltpu.VMEM((blocks, HEADS, HEAD, HEAD), F32)
    pieces = pltpu.VMEM((2, nz, rows, HEAD), F32)
    return pl.pallas_call(
        functools.partial(main_kernel, nz),
        out_shape=outs,
        in_specs=[hbm] * 3,
        out_specs=(vmem,) * len(outs),
        scratch_shapes=[
            pltpu.VMEM((tokens, width), F32),
            pltpu.VMEM((tokens, width), F32),
            pltpu.VMEM((tokens, width), F32),
            pltpu.VMEM((tokens, width), F32),
            pltpu.VMEM((blocks, HEADS, BLOCK, BLOCK), F32),
            pltpu.VMEM((2, blocks, HEADS, HEAD, BLOCK), BF16),
            pltpu.VMEM((2, blocks, HEADS, BLOCK, HEAD), BF16),
            pltpu.VMEM((2, blocks, HEADS, BLOCK, HEAD), BF16),
            square, square, square,
            pieces, pieces, pieces,
            pltpu.VMEM((2, nx, rows, HEAD), F32),
            pltpu.VMEM((2, ng, rows, HEAD), F32),
            pieces, pieces,
            dma, dma((blocks,)), dma((blocks,)),
            dma((2, nz)), dma((2, nz)), dma((2, nx)), dma((2, nx)),
            dma((2, ng)), dma((2, ng)), dma((2, nz)), dma((2, nz)),
        ],
        compiler_params=pltpu.CompilerParams(collective_id=0, has_side_effects=True, vmem_limit_bytes=63_400_000),
        name="steps",
    )(queries, keys, values)


def last_kernel(x_ref, near_ref, state_ref, out_ref):
    first = lax.axis_index("grp") * lax.axis_size("seq") + lax.axis_index("seq")
    first = (first * pl.num_programs(0) + pl.program_id(0)) * GROUP
    for c in range(GROUP // BLOCK):
        n = pl.program_id(0) * (GROUP // BLOCK) + c
        row = pl.ds(pl.multiple_of(n * BLOCK, BLOCK), BLOCK)
        place = (first + c * BLOCK + lax.broadcasted_iota(jnp.int32, (BLOCK, HEAD), 0)).astype(F32)
        scale = jnp.sqrt(place + 1.0)
        for h in range(HEADS):
            out = narrow(*halves(x_ref[row, lanes(h)]), state_ref[0, n, h], state_ref[1, n, h])
            out_ref[pl.ds(c * BLOCK, BLOCK), lanes(h)] = (out + near_ref[row, lanes(h)]) * scale


def last(*parts):
    tokens, width = parts[0].shape
    return pl.pallas_call(
        last_kernel,
        grid=(tokens // GROUP,),
        out_shape=jax.ShapeDtypeStruct((tokens, width), F32),
        in_specs=[pl.BlockSpec(memory_space=pltpu.VMEM)] * len(parts),
        out_specs=pl.BlockSpec((GROUP, width), lambda n: (n, 0)),
        compiler_params=pltpu.CompilerParams(vmem_limit_bytes=16 * 2**20),
        name="last",
    )(*parts)


def on_device(queries, keys, values):
    return last(*steps(queries, keys, values, ZDIM))


def solution(mesh):
    return jax.shard_map(
        on_device,
        mesh=mesh,
        in_specs=(P(("grp", "seq"), None), P(("grp", "seq"), None), P(("grp", "seq"), None)),
        out_specs=P(("grp", "seq"), None),
        check_vma=False,
    )
```

```python
import functools

import jax
import jax.numpy as jnp
from jax import lax
from jax.experimental import pallas as pl
from jax.experimental.pallas import tpu as pltpu
from jax.sharding import PartitionSpec as P

HEADS = 2
HEAD = 128
BLOCK = 256
ITERS = 4
ZDIM = 8
GROUP = 1024
AHEAD = 2
F32 = jnp.float32
BF16 = jnp.bfloat16
MESH = pl.DeviceIdType.MESH


def halves(x):
    hi = x.astype(BF16)
    return hi, (x - hi.astype(F32)).astype(BF16)


def cat(*xs, axis):
    return jnp.concatenate(xs, axis=axis)


def mm(a, b):
    return jnp.dot(a, b, preferred_element_type=F32)


def mmt(a, b):
    return lax.dot_general(a, b, (((0,), (0,)), ((), ())), preferred_element_type=F32)


def narrow(a_hi, a_lo, b_hi, b_lo):
    right = cat(cat(b_hi, b_lo, axis=1), cat(b_hi, jnp.zeros_like(b_lo), axis=1), axis=0)
    t = mm(cat(a_hi, a_lo, axis=1), right)
    return t[:, :HEAD] + t[:, HEAD:]


def scores_of(a_hi, a_lo, kt_hi, kt_lo):
    return mm(cat(a_hi, a_lo, axis=1), cat(kt_hi, kt_hi, axis=0)) + mm(a_hi, kt_lo)


def weighted(s, b_hi, b_lo):
    s_hi, s_lo = halves(s)
    t = mm(cat(s_hi, s_lo, axis=0), cat(b_hi, b_lo, axis=1))
    return t[:BLOCK, :HEAD] + t[:BLOCK, HEAD:] + t[BLOCK:, :HEAD]


def causal_mask():
    rows = lax.broadcasted_iota(jnp.int32, (BLOCK, BLOCK), 0)
    cols = lax.broadcasted_iota(jnp.int32, (BLOCK, BLOCK), 1)
    return cols <= rows


def lanes(h):
    return pl.ds(h * HEAD, HEAD)


def dots(a, b):
    return jnp.sum(a * b, axis=-1, keepdims=True)


def energy(a, b):
    return jnp.sum(a + (b[:, :HEAD] + b[:, HEAD:]), axis=-1, keepdims=True)


def main_kernel(
    nz, q_hbm, k_hbm, v_hbm, x_ref, near_ref, state_ref, near_s,
    qbuf, kbuf, vbuf, img, s_ref, kt, kh, vh, near_a, near_b,
    sums, zin, zpre, xin, gin, eout, e,
    qsem, ksem, vsem, zs, zr, xs, xr, gs, gr, es, er,
):
    blocks = kbuf.shape[0] // BLOCK
    rows = HEADS * HEAD // nz

    def span(b):
        return pl.ds(b * BLOCK, BLOCK)

    k_loads = [pltpu.make_async_copy(k_hbm.at[span(b)], kbuf.at[span(b)], ksem.at[b]) for b in range(blocks)]
    v_loads = [pltpu.make_async_copy(v_hbm.at[span(b)], vbuf.at[span(b)], vsem.at[b]) for b in range(blocks)]
    q_load = pltpu.make_async_copy(q_hbm, qbuf, qsem)
    for load in k_loads:
        load.start()
    g, s = lax.axis_index("grp"), lax.axis_index("seq")
    ng, nx = lax.axis_size("grp"), lax.axis_size("seq") // nz
    z, x = s % nz, s // nz

    def along_z(d):
        return {"grp": g, "seq": x * nz + (z + d) % nz}

    def along_x(d):
        return {"grp": g, "seq": ((x + d) % nx) * nz + z}

    def along_g(d):
        return {"grp": (g + d) % ng, "seq": s}

    barrier = pltpu.get_barrier_semaphore()
    partners = [along_z(d) for d in range(1, nz)] + [along_x(d) for d in range(1, nx)] + [along_g(d) for d in range(1, ng)]
    for partner in partners:
        pl.semaphore_signal(barrier, inc=1, device_id=partner, device_id_type=MESH)

    def remote(src, dst, send, recv, to):
        return pltpu.make_async_remote_copy(
            src_ref=src, dst_ref=dst, send_sem=send, recv_sem=recv, device_id=to, device_id_type=MESH)

    def landing(c):
        return state_ref if c else e

    def zcopy(c, d):
        return remote(sums.at[c, (z + d) % nz], zin.at[c, z], zs.at[c, d], zr.at[c, d], along_z(d))

    def xcopy(c, d):
        return remote(xin.at[c, x], xin.at[c, x], xs.at[c, d], xr.at[c, d], along_x(d))

    def gcopy(c, d):
        return remote(gin.at[c, g], gin.at[c, g], gs.at[c, d], gr.at[c, d], along_g(d))

    def ecopy(c, d):
        return remote(eout.at[c, (z + d) % nz], landing(c).at[z], es.at[c, d], er.at[c, d], along_z(d))

    far_first = sorted(range(1, nz), key=lambda d: -min(d, nz - d))
    half = nz // HEADS

    def keep_sums(c, parts):
        for h, part in enumerate(parts):
            sums[c, pl.ds(h * half, half)] = part.reshape(half, rows, HEAD)

    def send_sums(c):
        for d in far_first:
            zcopy(c, d).start()
        zin[c, z] = sums[c, z]

    total_a = [jnp.zeros((HEAD, HEAD), F32) for _ in range(HEADS)]
    total_b = [jnp.zeros((HEAD, HEAD), F32) for _ in range(HEADS)]
    for b in range(blocks):
        k_loads[b].wait()
        if b == blocks - 1:
            for load in v_loads + [q_load]:
                load.start()
        for h in range(HEADS):
            k_hi, k_lo = halves(kbuf[span(b), lanes(h)])
            kh[0, b, h] = k_hi
            kh[1, b, h] = k_lo
            wide = mmt(k_hi, cat(k_hi, k_lo, axis=1))
            near_a[b, h] = total_a[h]
            near_b[b, h] = total_b[h]
            total_a[h] = total_a[h] + (wide[:, :HEAD] + wide[:, HEAD:])
            total_b[h] = total_b[h] + wide[:, HEAD:]
    grams = [total_a[h] + total_b[h].T for h in range(HEADS)]
    pl.semaphore_wait(barrier, len(partners))
    keep_sums(0, grams)
    send_sums(0)

    total_s = [jnp.zeros((HEAD, HEAD), F32) for _ in range(HEADS)]
    for b in range(blocks):
        v_loads[b].wait()
        for h in range(HEADS):
            v_hi, v_lo = halves(vbuf[span(b), lanes(h)])
            vh[0, b, h] = v_hi
            vh[1, b, h] = v_lo
            wide = mmt(kh[0, b, h], cat(v_hi, v_lo, axis=1))
            near_s[b, h] = total_s[h]
            total_s[h] = total_s[h] + (wide[:, :HEAD] + wide[:, HEAD:] + mmt(kh[1, b, h], v_hi))
    keep_sums(1, total_s)

    q_load.wait()

    def local_part(b):
        causal = causal_mask()
        row = pl.ds(pl.multiple_of(b * BLOCK, BLOCK), BLOCK)
        for h in range(HEADS):
            q = qbuf[row, lanes(h)]
            q_hi, q_lo = halves(q)
            kt_hi, kt_lo = halves(kbuf[row, lanes(h)].T)
            kt[0, b, h] = kt_hi
            kt[1, b, h] = kt_lo
            scores = jnp.where(causal, scores_of(q_hi, q_lo, kt_hi, kt_lo), 0.0)
            s_ref[0, b, h] = scores
            gram = near_a[b, h] + near_b[b, h].T
            near_a[b, h] = gram
            near = weighted(scores, kh[0, b, h], kh[1, b, h])
            img[row, lanes(h)] = near + narrow(q_hi, q_lo, *halves(gram)) + q

    pl.loop(0, AHEAD)(local_part)

    zero = jnp.zeros((rows, HEAD), F32)
    held = {}

    def after_z(c):
        for d in range(1, nz):
            zcopy(c, d).wait_recv()
        run = zero
        for j in range(nz):
            zpre[c, j] = run
            run = run + zin[c, j]
        xin[c, x] = run
        for d in range(1, nx):
            xcopy(c, d).start()

    def after_x(c):
        for d in range(1, nx):
            xcopy(c, d).wait_recv()
        before, whole = zero, zero
        for j in range(nx):
            piece = xin[c, j]
            before = before + jnp.where(j < x, piece, 0.0)
            whole = whole + piece
        held[c] = before
        gin[c, g] = whole
        for d in range(1, ng):
            @pl.when(g + d < ng)
            def _():
                gcopy(c, d).start()

    def after_g(c):
        for d in range(1, ng):
            @pl.when(g - d >= 0)
            def _():
                gcopy(c, d).wait_recv()
        before = held[c] + lax.fori_loop(0, g, lambda j, acc: acc + gin[c, j], zero)
        for j in range(nz):
            eout[c, j] = zpre[c, j] + before
        for i in range(nz - 1):
            ecopy(c, (i + (i >= z).astype(jnp.int32) - z + nz) % nz).start()
        landing(c)[z] = eout[c, z]

    def solve_group(i):
        causal = causal_mask()
        work = []
        every = pl.ds(pl.multiple_of(i * GROUP, GROUP), GROUP)
        enter = [e[pl.ds(h * half, half)].reshape(HEAD, HEAD) for h in range(HEADS)]
        far = [narrow(*halves(qbuf[every, lanes(h)]), *halves(enter[h])) for h in range(HEADS)]
        for c in range(GROUP // BLOCK):
            for h in range(HEADS):
                n = i * (GROUP // BLOCK) + c
                row = pl.ds(pl.multiple_of(n * BLOCK, BLOCK), BLOCK)
                q = qbuf[row, lanes(h)]
                work.append(dict(
                    n=n, h=h, row=row, far=far[h][c * BLOCK : (c + 1) * BLOCK], gram=halves(enter[h] + near_a[n, h]),
                    r=q, p=q, rr=dots(q, q)))
        for step in range(ITERS - 1):
            images, scores = [], []
            for st in work:
                n, h = st["n"], st["h"]
                if step == 0:
                    scores.append(s_ref[0, n, h])
                    images.append(st["far"] + img[st["row"], lanes(h)])
                else:
                    p_hi, p_lo = halves(st["p"])
                    sc = jnp.where(causal, scores_of(p_hi, p_lo, kt[0, n, h], kt[1, n, h]), 0.0)
                    scores.append(sc)
                    images.append(narrow(p_hi, p_lo, *st["gram"]) + weighted(sc, kh[0, n, h], kh[1, n, h]) + st["p"])
            for st, image, sc in zip(work, images, scores):
                alpha = st["rr"] / dots(st["p"], image)
                st["acc"] = alpha * sc if step == 0 else st["acc"] + alpha * sc
                st["x"] = alpha * st["p"] if step == 0 else st["x"] + alpha * st["p"]
                st["r"] = st["r"] - alpha * image
                new = dots(st["r"], st["r"])
                st["p"] = st["r"] + new / st["rr"] * st["p"]
                st["rr"] = new
        for lo in range(0, len(work), 4):
            part = work[lo : lo + 4]
            scores, images, mixes = [], [], []
            for st in part:
                n, h = st["n"], st["h"]
                p_hi, p_lo = halves(st["p"])
                scores.append(jnp.where(causal, scores_of(p_hi, p_lo, kt[0, n, h], kt[1, n, h]), 0.0))
                images.append(narrow(p_hi, p_lo, *st["gram"]) + st["p"])
            for st, image, sc in zip(part, images, scores):
                n, h = st["n"], st["h"]
                alpha = st["rr"] / energy(st["p"] * image, sc * sc)
                st["x"] = st["x"] + alpha * st["p"]
                mix = st["acc"] + alpha * sc
                mixes.append(weighted(mix, vh[0, n, h], vh[1, n, h]))
            for st, mix in zip(part, mixes):
                x_ref[st["row"], lanes(st["h"])] = st["x"]
                near_ref[st["row"], lanes(st["h"])] = mix

    groups = blocks * BLOCK // GROUP
    send_sums(1)
    after_z(0)
    after_x(0)
    after_z(1)
    after_g(0)
    after_x(1)
    pl.loop(AHEAD, blocks)(local_part)
    after_g(1)
    for d in range(1, nz):
        ecopy(0, d).wait_recv()
    pl.loop(0, groups)(solve_group)
    for d in range(1, nz):
        ecopy(1, d).wait_recv()
    for c in range(2):
        for d in range(1, nz):
            zcopy(c, d).wait_send()
            ecopy(c, d).wait_send()
        for d in range(1, nx):
            xcopy(c, d).wait_send()
        for d in range(1, ng):
            @pl.when(g + d < ng)
            def _():
                gcopy(c, d).wait_send()


def steps(queries, keys, values, nz):
    tokens, width = keys.shape
    blocks = tokens // BLOCK
    nx, ng = lax.axis_size("seq") // nz, lax.axis_size("grp")
    rows = HEADS * HEAD // nz
    hbm = pl.BlockSpec(memory_space=pltpu.HBM)
    vmem = pl.BlockSpec(memory_space=pltpu.VMEM)
    dma = pltpu.SemaphoreType.DMA
    outs = (
        pltpu.VMEM((tokens, width), F32),
        pltpu.VMEM((tokens, width), F32),
        pltpu.VMEM((nz, rows, HEAD), F32),
        pltpu.VMEM((blocks, HEADS, HEAD, HEAD), F32),
    )
    square = pltpu.VMEM((blocks, HEADS, HEAD, HEAD), F32)
    pieces = pltpu.VMEM((2, nz, rows, HEAD), F32)
    return pl.pallas_call(
        functools.partial(main_kernel, nz),
        out_shape=outs,
        in_specs=[hbm] * 3,
        out_specs=(vmem,) * len(outs),
        scratch_shapes=[
            pltpu.VMEM((tokens, width), F32),
            pltpu.VMEM((tokens, width), F32),
            pltpu.VMEM((tokens, width), F32),
            pltpu.VMEM((tokens, width), F32),
            pltpu.VMEM((1, blocks, HEADS, BLOCK, BLOCK), F32),
            pltpu.VMEM((2, blocks, HEADS, HEAD, BLOCK), BF16),
            pltpu.VMEM((2, blocks, HEADS, BLOCK, HEAD), BF16),
            pltpu.VMEM((2, blocks, HEADS, BLOCK, HEAD), BF16),
            square, square,
            pieces, pieces, pieces,
            pltpu.VMEM((2, nx, rows, HEAD), F32),
            pltpu.VMEM((2, ng, rows, HEAD), F32),
            pieces, pltpu.VMEM((nz, rows, HEAD), F32),
            dma, dma((blocks,)), dma((blocks,)),
            dma((2, nz)), dma((2, nz)), dma((2, nx)), dma((2, nx)),
            dma((2, ng)), dma((2, ng)), dma((2, nz)), dma((2, nz)),
        ],
        compiler_params=pltpu.CompilerParams(collective_id=0, has_side_effects=True, vmem_limit_bytes=63_300_000),
        name="steps",
    )(queries, keys, values)


def last_kernel(x_ref, near_ref, state_ref, near_s, out_ref):
    first = lax.axis_index("grp") * lax.axis_size("seq") + lax.axis_index("seq")
    first = (first * pl.num_programs(0) + pl.program_id(0)) * GROUP
    for c in range(GROUP // BLOCK):
        n = pl.program_id(0) * (GROUP // BLOCK) + c
        row = pl.ds(pl.multiple_of(n * BLOCK, BLOCK), BLOCK)
        place = (first + c * BLOCK + lax.broadcasted_iota(jnp.int32, (BLOCK, HEAD), 0)).astype(F32)
        scale = jnp.sqrt(place + 1.0)
        for h in range(HEADS):
            half = state_ref.shape[0] // HEADS
            state = halves(state_ref[pl.ds(h * half, half)].reshape(HEAD, HEAD) + near_s[n, h])
            out = narrow(*halves(x_ref[row, lanes(h)]), *state)
            out_ref[pl.ds(c * BLOCK, BLOCK), lanes(h)] = (out + near_ref[row, lanes(h)]) * scale


def last(*parts):
    tokens, width = parts[0].shape
    return pl.pallas_call(
        last_kernel,
        grid=(tokens // GROUP,),
        out_shape=jax.ShapeDtypeStruct((tokens, width), F32),
        in_specs=[pl.BlockSpec(memory_space=pltpu.VMEM)] * len(parts),
        out_specs=pl.BlockSpec((GROUP, width), lambda n: (n, 0)),
        compiler_params=pltpu.CompilerParams(vmem_limit_bytes=16 * 2**20),
        name="last",
    )(*parts)


def on_device(queries, keys, values):
    return last(*steps(queries, keys, values, ZDIM))


def solution(mesh):
    return jax.shard_map(
        on_device,
        mesh=mesh,
        in_specs=(P(("grp", "seq"), None), P(("grp", "seq"), None), P(("grp", "seq"), None)),
        out_specs=P(("grp", "seq"), None),
        check_vma=False,
    )
```

```python
import functools

import jax
import jax.numpy as jnp
from jax import lax
from jax.experimental import pallas as pl
from jax.experimental.pallas import tpu as pltpu
from jax.sharding import PartitionSpec as P

HEADS = 2
HEAD = 128
BLOCK = 256
ITERS = 4
ZDIM = 8
GROUP = 1024
AHEAD = 2
F32 = jnp.float32
BF16 = jnp.bfloat16
MESH = pl.DeviceIdType.MESH


def halves(x):
    hi = x.astype(BF16)
    return hi, (x - hi.astype(F32)).astype(BF16)


def cat(*xs, axis):
    return jnp.concatenate(xs, axis=axis)


def mm(a, b):
    return jnp.dot(a, b, preferred_element_type=F32)


def mmt(a, b):
    return lax.dot_general(a, b, (((0,), (0,)), ((), ())), preferred_element_type=F32)


def narrow(a_hi, a_lo, b_hi, b_lo):
    right = cat(cat(b_hi, b_lo, axis=1), cat(b_hi, jnp.zeros_like(b_lo), axis=1), axis=0)
    t = mm(cat(a_hi, a_lo, axis=1), right)
    return t[:, :HEAD] + t[:, HEAD:]


def scores_of(a_hi, a_lo, kt_hi, kt_lo):
    return mm(cat(a_hi, a_lo, axis=1), cat(kt_hi, kt_hi, axis=0)) + mm(a_hi, kt_lo)


def weighted(s, b_hi, b_lo):
    s_hi, s_lo = halves(s)
    t = mm(cat(s_hi, s_lo, axis=0), cat(b_hi, b_lo, axis=1))
    return t[:BLOCK, :HEAD] + t[:BLOCK, HEAD:] + t[BLOCK:, :HEAD]


def causal_mask():
    rows = lax.broadcasted_iota(jnp.int32, (BLOCK, BLOCK), 0)
    cols = lax.broadcasted_iota(jnp.int32, (BLOCK, BLOCK), 1)
    return cols <= rows


def lanes(h):
    return pl.ds(h * HEAD, HEAD)


def dots(a, b):
    return jnp.sum(a * b, axis=-1, keepdims=True)


def energy(a, b):
    return jnp.sum(a + (b[:, :HEAD] + b[:, HEAD:]), axis=-1, keepdims=True)


def main_kernel(
    nz, q_hbm, k_hbm, v_hbm, x_ref, near_ref, state_ref, near_s,
    qbuf, kbuf, vbuf, img, s_ref, kt, kh, vh, near_a, near_b,
    sums, zin, zpre, xin, gin, eout, e,
    qsem, ksem, vsem, zs, zr, xs, xr, gs, gr, es, er,
):
    blocks = kbuf.shape[0] // BLOCK
    rows = HEADS * HEAD // nz

    def span(b):
        return pl.ds(b * BLOCK, BLOCK)

    k_loads = [pltpu.make_async_copy(k_hbm.at[span(b)], kbuf.at[span(b)], ksem.at[b]) for b in range(blocks)]
    v_loads = [pltpu.make_async_copy(v_hbm.at[span(b)], vbuf.at[span(b)], vsem.at[b]) for b in range(blocks)]
    q_load = pltpu.make_async_copy(q_hbm, qbuf, qsem)
    for load in k_loads:
        load.start()
    g, s = lax.axis_index("grp"), lax.axis_index("seq")
    ng, nx = lax.axis_size("grp"), lax.axis_size("seq") // nz
    z, x = s % nz, s // nz

    def along_z(d):
        return {"grp": g, "seq": x * nz + (z + d) % nz}

    def along_x(d):
        return {"grp": g, "seq": ((x + d) % nx) * nz + z}

    def along_g(d):
        return {"grp": (g + d) % ng, "seq": s}

    barrier = pltpu.get_barrier_semaphore()
    partners = [along_z(d) for d in range(1, nz)] + [along_x(d) for d in range(1, nx)] + [along_g(d) for d in range(1, ng)]
    for partner in partners:
        pl.semaphore_signal(barrier, inc=1, device_id=partner, device_id_type=MESH)

    def remote(src, dst, send, recv, to):
        return pltpu.make_async_remote_copy(
            src_ref=src, dst_ref=dst, send_sem=send, recv_sem=recv, device_id=to, device_id_type=MESH)

    def landing(c):
        return state_ref if c else e

    def zcopy(c, d):
        return remote(sums.at[c, (z + d) % nz], zin.at[c, z], zs.at[c, d], zr.at[c, d], along_z(d))

    def xcopy(c, d):
        return remote(xin.at[c, x], xin.at[c, x], xs.at[c, d], xr.at[c, d], along_x(d))

    def gcopy(c, d):
        return remote(gin.at[c, g], gin.at[c, g], gs.at[c, d], gr.at[c, d], along_g(d))

    def ecopy(c, d):
        return remote(eout.at[c, (z + d) % nz], landing(c).at[z], es.at[c, d], er.at[c, d], along_z(d))

    far_first = sorted(range(1, nz), key=lambda d: -min(d, nz - d))
    half = nz // HEADS

    def keep_sums(c, parts):
        for h, part in enumerate(parts):
            sums[c, pl.ds(h * half, half)] = part.reshape(half, rows, HEAD)

    def send_sums(c):
        for d in far_first:
            zcopy(c, d).start()
        zin[c, z] = sums[c, z]

    total_a = [jnp.zeros((HEAD, HEAD), F32) for _ in range(HEADS)]
    total_b = [jnp.zeros((HEAD, HEAD), F32) for _ in range(HEADS)]
    for b in range(blocks):
        k_loads[b].wait()
        if b == blocks - 1:
            for load in v_loads + [q_load]:
                load.start()
        for h in range(HEADS):
            k_hi, k_lo = halves(kbuf[span(b), lanes(h)])
            kh[0, b, h] = k_hi
            kh[1, b, h] = k_lo
            wide = mmt(k_hi, cat(k_hi, k_lo, axis=1))
            near_a[b, h] = total_a[h]
            near_b[b, h] = total_b[h]
            total_a[h] = total_a[h] + (wide[:, :HEAD] + wide[:, HEAD:])
            total_b[h] = total_b[h] + wide[:, HEAD:]
    grams = [total_a[h] + total_b[h].T for h in range(HEADS)]
    pl.semaphore_wait(barrier, len(partners))
    keep_sums(0, grams)
    send_sums(0)

    total_s = [jnp.zeros((HEAD, HEAD), F32) for _ in range(HEADS)]
    for b in range(blocks):
        v_loads[b].wait()
        for h in range(HEADS):
            v_hi, v_lo = halves(vbuf[span(b), lanes(h)])
            vh[0, b, h] = v_hi
            vh[1, b, h] = v_lo
            wide = mmt(kh[0, b, h], cat(v_hi, v_lo, axis=1))
            near_s[b, h] = total_s[h]
            total_s[h] = total_s[h] + (wide[:, :HEAD] + wide[:, HEAD:] + mmt(kh[1, b, h], v_hi))
    keep_sums(1, total_s)

    q_load.wait()

    def local_part(b):
        causal = causal_mask()
        row = pl.ds(pl.multiple_of(b * BLOCK, BLOCK), BLOCK)
        for h in range(HEADS):
            q = qbuf[row, lanes(h)]
            q_hi, q_lo = halves(q)
            kt_hi, kt_lo = halves(kbuf[row, lanes(h)].T)
            kt[0, b, h] = kt_hi
            kt[1, b, h] = kt_lo
            scores = jnp.where(causal, scores_of(q_hi, q_lo, kt_hi, kt_lo), 0.0)
            s_ref[0, b, h] = scores
            gram = near_a[b, h] + near_b[b, h].T
            near_a[b, h] = gram
            near = weighted(scores, kh[0, b, h], kh[1, b, h])
            img[row, lanes(h)] = near + narrow(q_hi, q_lo, *halves(gram)) + q

    pl.loop(0, AHEAD)(local_part)

    zero = jnp.zeros((rows, HEAD), F32)
    held = {}

    def after_z(c):
        for d in range(1, nz):
            zcopy(c, d).wait_recv()
        run = zero
        for j in range(nz):
            zpre[c, j] = run
            run = run + zin[c, j]
        xin[c, x] = run
        for d in sorted(range(1, nx), key=lambda d: -min(d, nx - d)):
            xcopy(c, d).start()

    def after_x(c):
        for d in range(1, nx):
            xcopy(c, d).wait_recv()
        before, whole = zero, zero
        for j in range(nx):
            piece = xin[c, j]
            before = before + jnp.where(j < x, piece, 0.0)
            whole = whole + piece
        held[c] = before
        gin[c, g] = whole
        for d in sorted(range(1, ng), key=lambda d: -min(d, ng - d)):
            @pl.when(g + d < ng)
            def _():
                gcopy(c, d).start()

    def after_g(c):
        for d in range(1, ng):
            @pl.when(g - d >= 0)
            def _():
                gcopy(c, d).wait_recv()
        before = held[c] + lax.fori_loop(0, g, lambda j, acc: acc + gin[c, j], zero)
        for j in range(nz):
            eout[c, j] = zpre[c, j] + before
        for i in range(nz - 1):
            ecopy(c, (i + (i >= z).astype(jnp.int32) - z + nz) % nz).start()
        landing(c)[z] = eout[c, z]

    def solve_group(i):
        causal = causal_mask()
        work = []
        every = pl.ds(pl.multiple_of(i * GROUP, GROUP), GROUP)
        enter = [e[pl.ds(h * half, half)].reshape(HEAD, HEAD) for h in range(HEADS)]
        far = [narrow(*halves(qbuf[every, lanes(h)]), *halves(enter[h])) for h in range(HEADS)]
        for c in range(GROUP // BLOCK):
            for h in range(HEADS):
                n = i * (GROUP // BLOCK) + c
                row = pl.ds(pl.multiple_of(n * BLOCK, BLOCK), BLOCK)
                q = qbuf[row, lanes(h)]
                work.append(dict(
                    n=n, h=h, row=row, far=far[h][c * BLOCK : (c + 1) * BLOCK], gram=halves(enter[h] + near_a[n, h]),
                    r=q, p=q, rr=dots(q, q)))
        for step in range(ITERS - 1):
            images, scores = [], []
            for st in work:
                n, h = st["n"], st["h"]
                if step == 0:
                    scores.append(s_ref[0, n, h])
                    images.append(st["far"] + img[st["row"], lanes(h)])
                else:
                    p_hi, p_lo = halves(st["p"])
                    sc = jnp.where(causal, scores_of(p_hi, p_lo, kt[0, n, h], kt[1, n, h]), 0.0)
                    scores.append(sc)
                    images.append(narrow(p_hi, p_lo, *st["gram"]) + weighted(sc, kh[0, n, h], kh[1, n, h]) + st["p"])
            for st, image, sc in zip(work, images, scores):
                alpha = st["rr"] / dots(st["p"], image)
                st["acc"] = alpha * sc if step == 0 else st["acc"] + alpha * sc
                st["x"] = alpha * st["p"] if step == 0 else st["x"] + alpha * st["p"]
                st["r"] = st["r"] - alpha * image
                new = dots(st["r"], st["r"])
                st["p"] = st["r"] + new / st["rr"] * st["p"]
                st["rr"] = new
        for lo in range(0, len(work), 4):
            part = work[lo : lo + 4]
            scores, images, mixes = [], [], []
            for st in part:
                n, h = st["n"], st["h"]
                p_hi, p_lo = halves(st["p"])
                scores.append(jnp.where(causal, scores_of(p_hi, p_lo, kt[0, n, h], kt[1, n, h]), 0.0))
                images.append(narrow(p_hi, p_lo, *st["gram"]) + st["p"])
            for st, image, sc in zip(part, images, scores):
                n, h = st["n"], st["h"]
                alpha = st["rr"] / energy(st["p"] * image, sc * sc)
                st["x"] = st["x"] + alpha * st["p"]
                mix = st["acc"] + alpha * sc
                mixes.append(weighted(mix, vh[0, n, h], vh[1, n, h]))
            for st, mix in zip(part, mixes):
                x_ref[st["row"], lanes(st["h"])] = st["x"]
                near_ref[st["row"], lanes(st["h"])] = mix

    groups = blocks * BLOCK // GROUP
    send_sums(1)
    after_z(0)
    after_x(0)
    after_z(1)
    after_g(0)
    after_x(1)
    pl.loop(AHEAD, blocks)(local_part)
    after_g(1)
    for c in range(2):
        for d in range(1, nz):
            zcopy(c, d).wait_send()
        for d in range(1, nx):
            xcopy(c, d).wait_send()
        for d in range(1, ng):
            @pl.when(g + d < ng)
            def _():
                gcopy(c, d).wait_send()
    for d in range(1, nz):
        ecopy(0, d).wait_recv()
    pl.loop(0, groups)(solve_group)
    for d in range(1, nz):
        ecopy(1, d).wait_recv()
    for c in range(2):
        for d in range(1, nz):
            ecopy(c, d).wait_send()


def steps(queries, keys, values, nz):
    tokens, width = keys.shape
    blocks = tokens // BLOCK
    nx, ng = lax.axis_size("seq") // nz, lax.axis_size("grp")
    rows = HEADS * HEAD // nz
    hbm = pl.BlockSpec(memory_space=pltpu.HBM)
    vmem = pl.BlockSpec(memory_space=pltpu.VMEM)
    dma = pltpu.SemaphoreType.DMA
    outs = (
        pltpu.VMEM((tokens, width), F32),
        pltpu.VMEM((tokens, width), F32),
        pltpu.VMEM((nz, rows, HEAD), F32),
        pltpu.VMEM((blocks, HEADS, HEAD, HEAD), F32),
    )
    square = pltpu.VMEM((blocks, HEADS, HEAD, HEAD), F32)
    pieces = pltpu.VMEM((2, nz, rows, HEAD), F32)
    return pl.pallas_call(
        functools.partial(main_kernel, nz),
        out_shape=outs,
        in_specs=[hbm] * 3,
        out_specs=(vmem,) * len(outs),
        scratch_shapes=[
            pltpu.VMEM((tokens, width), F32),
            pltpu.VMEM((tokens, width), F32),
            pltpu.VMEM((tokens, width), F32),
            pltpu.VMEM((tokens, width), F32),
            pltpu.VMEM((1, blocks, HEADS, BLOCK, BLOCK), F32),
            pltpu.VMEM((2, blocks, HEADS, HEAD, BLOCK), BF16),
            pltpu.VMEM((2, blocks, HEADS, BLOCK, HEAD), BF16),
            pltpu.VMEM((2, blocks, HEADS, BLOCK, HEAD), BF16),
            square, square,
            pieces, pieces, pieces,
            pltpu.VMEM((2, nx, rows, HEAD), F32),
            pltpu.VMEM((2, ng, rows, HEAD), F32),
            pieces, pltpu.VMEM((nz, rows, HEAD), F32),
            dma, dma((blocks,)), dma((blocks,)),
            dma((2, nz)), dma((2, nz)), dma((2, nx)), dma((2, nx)),
            dma((2, ng)), dma((2, ng)), dma((2, nz)), dma((2, nz)),
        ],
        compiler_params=pltpu.CompilerParams(collective_id=0, has_side_effects=True, vmem_limit_bytes=63_300_000),
        name="steps",
    )(queries, keys, values)


def last_kernel(x_ref, near_ref, state_ref, near_s, out_ref):
    first = lax.axis_index("grp") * lax.axis_size("seq") + lax.axis_index("seq")
    first = (first * pl.num_programs(0) + pl.program_id(0)) * GROUP
    for c in range(GROUP // BLOCK):
        n = pl.program_id(0) * (GROUP // BLOCK) + c
        row = pl.ds(pl.multiple_of(n * BLOCK, BLOCK), BLOCK)
        place = (first + c * BLOCK + lax.broadcasted_iota(jnp.int32, (BLOCK, HEAD), 0)).astype(F32)
        scale = jnp.sqrt(place + 1.0)
        for h in range(HEADS):
            half = state_ref.shape[0] // HEADS
            state = halves(state_ref[pl.ds(h * half, half)].reshape(HEAD, HEAD) + near_s[n, h])
            out = narrow(*halves(x_ref[row, lanes(h)]), *state)
            out_ref[pl.ds(c * BLOCK, BLOCK), lanes(h)] = (out + near_ref[row, lanes(h)]) * scale


def last(*parts):
    tokens, width = parts[0].shape
    return pl.pallas_call(
        last_kernel,
        grid=(tokens // GROUP,),
        out_shape=jax.ShapeDtypeStruct((tokens, width), F32),
        in_specs=[pl.BlockSpec(memory_space=pltpu.VMEM)] * len(parts),
        out_specs=pl.BlockSpec((GROUP, width), lambda n: (n, 0)),
        compiler_params=pltpu.CompilerParams(vmem_limit_bytes=16 * 2**20),
        name="last",
    )(*parts)


def on_device(queries, keys, values):
    return last(*steps(queries, keys, values, ZDIM))


def solution(mesh):
    return jax.shard_map(
        on_device,
        mesh=mesh,
        in_specs=(P(("grp", "seq"), None), P(("grp", "seq"), None), P(("grp", "seq"), None)),
        out_specs=P(("grp", "seq"), None),
        check_vma=False,
    )
```

```python
import functools

import jax
import jax.numpy as jnp
from jax import lax
from jax.experimental import pallas as pl
from jax.experimental.pallas import tpu as pltpu
from jax.sharding import PartitionSpec as P

HEADS = 2
HEAD = 128
BLOCK = 256
ITERS = 4
ZDIM = 8
GROUP = 1024
AHEAD = 2
F32 = jnp.float32
BF16 = jnp.bfloat16
MESH = pl.DeviceIdType.MESH


def halves(x):
    hi = x.astype(BF16)
    return hi, (x - hi.astype(F32)).astype(BF16)


def cat(*xs, axis):
    return jnp.concatenate(xs, axis=axis)


def mm(a, b):
    return jnp.dot(a, b, preferred_element_type=F32)


def mmt(a, b):
    return lax.dot_general(a, b, (((0,), (0,)), ((), ())), preferred_element_type=F32)


def narrow(a_hi, a_lo, b_hi, b_lo):
    right = cat(cat(b_hi, b_lo, axis=1), cat(b_hi, jnp.zeros_like(b_lo), axis=1), axis=0)
    t = mm(cat(a_hi, a_lo, axis=1), right)
    return t[:, :HEAD] + t[:, HEAD:]


def scores_of(a_hi, a_lo, kt_hi, kt_lo):
    return mm(cat(a_hi, a_lo, axis=1), cat(kt_hi, kt_hi, axis=0)) + mm(a_hi, kt_lo)


def weighted(s, b_hi, b_lo):
    s_hi, s_lo = halves(s)
    t = mm(cat(s_hi, s_lo, axis=0), cat(b_hi, b_lo, axis=1))
    return t[:BLOCK, :HEAD] + t[:BLOCK, HEAD:] + t[BLOCK:, :HEAD]


def causal_mask():
    rows = lax.broadcasted_iota(jnp.int32, (BLOCK, BLOCK), 0)
    cols = lax.broadcasted_iota(jnp.int32, (BLOCK, BLOCK), 1)
    return cols <= rows


def lanes(h):
    return pl.ds(h * HEAD, HEAD)


def dots(a, b):
    return jnp.sum(a * b, axis=-1, keepdims=True)


def energy(a, b):
    return jnp.sum(a + (b[:, :HEAD] + b[:, HEAD:]), axis=-1, keepdims=True)


def main_kernel(
    nz, q_hbm, k_hbm, v_hbm, x_ref, near_ref, state_ref, near_s,
    qbuf, qh, kbuf, vbuf, img, s_ref, kt, kh, vh, near_a, near_b,
    sums, zin, zpre, xin, gin, eout, e,
    qsem, ksem, vsem, zs, zr, xs, xr, gs, gr, es, er,
):
    blocks = kbuf.shape[0] // BLOCK
    rows = HEADS * HEAD // nz

    def span(b):
        return pl.ds(b * BLOCK, BLOCK)

    k_loads = [pltpu.make_async_copy(k_hbm.at[span(b)], kbuf.at[span(b)], ksem.at[b]) for b in range(blocks)]
    v_loads = [pltpu.make_async_copy(v_hbm.at[span(b)], vbuf.at[span(b)], vsem.at[b]) for b in range(blocks)]
    q_load = pltpu.make_async_copy(q_hbm, qbuf, qsem)
    for load in k_loads:
        load.start()
    g, s = lax.axis_index("grp"), lax.axis_index("seq")
    ng, nx = lax.axis_size("grp"), lax.axis_size("seq") // nz
    z, x = s % nz, s // nz

    def along_z(d):
        return {"grp": g, "seq": x * nz + (z + d) % nz}

    def along_x(d):
        return {"grp": g, "seq": ((x + d) % nx) * nz + z}

    def along_g(d):
        return {"grp": (g + d) % ng, "seq": s}

    barrier = pltpu.get_barrier_semaphore()
    partners = [along_z(d) for d in range(1, nz)] + [along_x(d) for d in range(1, nx)] + [along_g(d) for d in range(1, ng)]
    for partner in partners:
        pl.semaphore_signal(barrier, inc=1, device_id=partner, device_id_type=MESH)

    def remote(src, dst, send, recv, to):
        return pltpu.make_async_remote_copy(
            src_ref=src, dst_ref=dst, send_sem=send, recv_sem=recv, device_id=to, device_id_type=MESH)

    def landing(c):
        return state_ref if c else e

    def zcopy(c, d):
        return remote(sums.at[c, (z + d) % nz], zin.at[c, z], zs.at[c, d], zr.at[c, d], along_z(d))

    def xcopy(c, d):
        return remote(xin.at[c, x], xin.at[c, x], xs.at[c, d], xr.at[c, d], along_x(d))

    def gcopy(c, d):
        return remote(gin.at[c, g], gin.at[c, g], gs.at[c, d], gr.at[c, d], along_g(d))

    def ecopy(c, d):
        return remote(eout.at[c, (z + d) % nz], landing(c).at[z], es.at[c, d], er.at[c, d], along_z(d))

    far_first = sorted(range(1, nz), key=lambda d: -min(d, nz - d))
    half = nz // HEADS

    def keep_sums(c, parts):
        for h, part in enumerate(parts):
            sums[c, pl.ds(h * half, half)] = part.reshape(half, rows, HEAD)

    def send_sums(c):
        for d in far_first:
            zcopy(c, d).start()
        zin[c, z] = sums[c, z]

    total_a = [jnp.zeros((HEAD, HEAD), F32) for _ in range(HEADS)]
    total_b = [jnp.zeros((HEAD, HEAD), F32) for _ in range(HEADS)]
    for b in range(blocks):
        k_loads[b].wait()
        if b == blocks - 1:
            for load in v_loads + [q_load]:
                load.start()
        for h in range(HEADS):
            k_hi, k_lo = halves(kbuf[span(b), lanes(h)])
            kh[0, b, h] = k_hi
            kh[1, b, h] = k_lo
            wide = mmt(k_hi, cat(k_hi, k_lo, axis=1))
            near_a[b, h] = total_a[h]
            near_b[b, h] = total_b[h]
            total_a[h] = total_a[h] + (wide[:, :HEAD] + wide[:, HEAD:])
            total_b[h] = total_b[h] + wide[:, HEAD:]
    grams = [total_a[h] + total_b[h].T for h in range(HEADS)]
    pl.semaphore_wait(barrier, len(partners))
    keep_sums(0, grams)
    send_sums(0)

    total_s = [jnp.zeros((HEAD, HEAD), F32) for _ in range(HEADS)]
    for b in range(blocks):
        v_loads[b].wait()
        for h in range(HEADS):
            v_hi, v_lo = halves(vbuf[span(b), lanes(h)])
            vh[0, b, h] = v_hi
            vh[1, b, h] = v_lo
            wide = mmt(kh[0, b, h], cat(v_hi, v_lo, axis=1))
            near_s[b, h] = total_s[h]
            total_s[h] = total_s[h] + (wide[:, :HEAD] + wide[:, HEAD:] + mmt(kh[1, b, h], v_hi))
    keep_sums(1, total_s)

    q_load.wait()

    def local_part(b):
        causal = causal_mask()
        row = pl.ds(pl.multiple_of(b * BLOCK, BLOCK), BLOCK)
        for h in range(HEADS):
            q = qbuf[row, lanes(h)]
            q_hi, q_lo = halves(q)
            qh[0, row, lanes(h)] = q_hi
            qh[1, row, lanes(h)] = q_lo
            kt_hi, kt_lo = halves(kbuf[row, lanes(h)].T)
            kt[0, b, h] = kt_hi
            kt[1, b, h] = kt_lo
            scores = jnp.where(causal, scores_of(q_hi, q_lo, kt_hi, kt_lo), 0.0)
            s_ref[0, b, h] = scores
            gram = near_a[b, h] + near_b[b, h].T
            near_a[b, h] = gram
            near = weighted(scores, kh[0, b, h], kh[1, b, h])
            img[row, lanes(h)] = near + narrow(q_hi, q_lo, *halves(gram)) + q

    pl.loop(0, AHEAD)(local_part)

    zero = jnp.zeros((rows, HEAD), F32)
    held = {}

    def after_z(c):
        for d in range(1, nz):
            zcopy(c, d).wait_recv()
        run = zero
        for j in range(nz):
            zpre[c, j] = run
            run = run + zin[c, j]
        xin[c, x] = run
        for d in sorted(range(1, nx), key=lambda d: -min(d, nx - d)):
            xcopy(c, d).start()

    def after_x(c):
        for d in range(1, nx):
            xcopy(c, d).wait_recv()
        before, whole = zero, zero
        for j in range(nx):
            piece = xin[c, j]
            before = before + jnp.where(j < x, piece, 0.0)
            whole = whole + piece
        held[c] = before
        gin[c, g] = whole
        for d in sorted(range(1, ng), key=lambda d: -min(d, ng - d)):
            @pl.when(g + d < ng)
            def _():
                gcopy(c, d).start()

    def after_g(c):
        for d in range(1, ng):
            @pl.when(g - d >= 0)
            def _():
                gcopy(c, d).wait_recv()
        before = held[c] + lax.fori_loop(0, g, lambda j, acc: acc + gin[c, j], zero)
        for j in range(nz):
            eout[c, j] = zpre[c, j] + before
        for i in range(nz - 1):
            ecopy(c, (i + (i >= z).astype(jnp.int32) - z + nz) % nz).start()
        landing(c)[z] = eout[c, z]

    def solve_group(i):
        causal = causal_mask()
        work = []
        every = pl.ds(pl.multiple_of(i * GROUP, GROUP), GROUP)
        enter = [e[pl.ds(h * half, half)].reshape(HEAD, HEAD) for h in range(HEADS)]
        far = [narrow(qh[0, every, lanes(h)], qh[1, every, lanes(h)], *halves(enter[h])) for h in range(HEADS)]
        for c in range(GROUP // BLOCK):
            for h in range(HEADS):
                n = i * (GROUP // BLOCK) + c
                row = pl.ds(pl.multiple_of(n * BLOCK, BLOCK), BLOCK)
                q = qbuf[row, lanes(h)]
                work.append(dict(
                    n=n, h=h, row=row, far=far[h][c * BLOCK : (c + 1) * BLOCK], gram=halves(enter[h] + near_a[n, h]),
                    r=q, p=q, rr=dots(q, q)))
        for step in range(ITERS - 1):
            images, scores = [], []
            for st in work:
                n, h = st["n"], st["h"]
                if step == 0:
                    scores.append(s_ref[0, n, h])
                    images.append(st["far"] + img[st["row"], lanes(h)])
                else:
                    p_hi, p_lo = halves(st["p"])
                    sc = jnp.where(causal, scores_of(p_hi, p_lo, kt[0, n, h], kt[1, n, h]), 0.0)
                    scores.append(sc)
                    images.append(narrow(p_hi, p_lo, *st["gram"]) + weighted(sc, kh[0, n, h], kh[1, n, h]) + st["p"])
            for st, image, sc in zip(work, images, scores):
                alpha = st["rr"] / dots(st["p"], image)
                st["acc"] = alpha * sc if step == 0 else st["acc"] + alpha * sc
                st["x"] = alpha * st["p"] if step == 0 else st["x"] + alpha * st["p"]
                st["r"] = st["r"] - alpha * image
                new = dots(st["r"], st["r"])
                st["p"] = st["r"] + new / st["rr"] * st["p"]
                st["rr"] = new
        for lo in range(0, len(work), 4):
            part = work[lo : lo + 4]
            scores, images, mixes = [], [], []
            for st in part:
                n, h = st["n"], st["h"]
                p_hi, p_lo = halves(st["p"])
                scores.append(jnp.where(causal, scores_of(p_hi, p_lo, kt[0, n, h], kt[1, n, h]), 0.0))
                images.append(narrow(p_hi, p_lo, *st["gram"]) + st["p"])
            for st, image, sc in zip(part, images, scores):
                n, h = st["n"], st["h"]
                alpha = st["rr"] / energy(st["p"] * image, sc * sc)
                st["x"] = st["x"] + alpha * st["p"]
                mix = st["acc"] + alpha * sc
                mixes.append(weighted(mix, vh[0, n, h], vh[1, n, h]))
            for st, mix in zip(part, mixes):
                x_ref[st["row"], lanes(st["h"])] = st["x"]
                near_ref[st["row"], lanes(st["h"])] = mix

    groups = blocks * BLOCK // GROUP
    send_sums(1)
    after_z(0)
    after_x(0)
    after_z(1)
    after_g(0)
    after_x(1)
    pl.loop(AHEAD, blocks)(local_part)
    after_g(1)
    for c in range(2):
        for d in range(1, nz):
            zcopy(c, d).wait_send()
        for d in range(1, nx):
            xcopy(c, d).wait_send()
        for d in range(1, ng):
            @pl.when(g + d < ng)
            def _():
                gcopy(c, d).wait_send()
    for d in range(1, nz):
        ecopy(0, d).wait_recv()
    pl.loop(0, groups)(solve_group)
    for d in range(1, nz):
        ecopy(1, d).wait_recv()
    for c in range(2):
        for d in range(1, nz):
            ecopy(c, d).wait_send()


def steps(queries, keys, values, nz):
    tokens, width = keys.shape
    blocks = tokens // BLOCK
    nx, ng = lax.axis_size("seq") // nz, lax.axis_size("grp")
    rows = HEADS * HEAD // nz
    hbm = pl.BlockSpec(memory_space=pltpu.HBM)
    vmem = pl.BlockSpec(memory_space=pltpu.VMEM)
    dma = pltpu.SemaphoreType.DMA
    outs = (
        pltpu.VMEM((tokens, width), F32),
        pltpu.VMEM((tokens, width), F32),
        pltpu.VMEM((nz, rows, HEAD), F32),
        pltpu.VMEM((blocks, HEADS, HEAD, HEAD), F32),
    )
    square = pltpu.VMEM((blocks, HEADS, HEAD, HEAD), F32)
    pieces = pltpu.VMEM((2, nz, rows, HEAD), F32)
    return pl.pallas_call(
        functools.partial(main_kernel, nz),
        out_shape=outs,
        in_specs=[hbm] * 3,
        out_specs=(vmem,) * len(outs),
        scratch_shapes=[
            pltpu.VMEM((tokens, width), F32),
            pltpu.VMEM((2, tokens, width), BF16),
            pltpu.VMEM((tokens, width), F32),
            pltpu.VMEM((tokens, width), F32),
            pltpu.VMEM((tokens, width), F32),
            pltpu.VMEM((1, blocks, HEADS, BLOCK, BLOCK), F32),
            pltpu.VMEM((2, blocks, HEADS, HEAD, BLOCK), BF16),
            pltpu.VMEM((2, blocks, HEADS, BLOCK, HEAD), BF16),
            pltpu.VMEM((2, blocks, HEADS, BLOCK, HEAD), BF16),
            square, square,
            pieces, pieces, pieces,
            pltpu.VMEM((2, nx, rows, HEAD), F32),
            pltpu.VMEM((2, ng, rows, HEAD), F32),
            pieces, pltpu.VMEM((nz, rows, HEAD), F32),
            dma, dma((blocks,)), dma((blocks,)),
            dma((2, nz)), dma((2, nz)), dma((2, nx)), dma((2, nx)),
            dma((2, ng)), dma((2, ng)), dma((2, nz)), dma((2, nz)),
        ],
        compiler_params=pltpu.CompilerParams(collective_id=0, has_side_effects=True, vmem_limit_bytes=63_300_000),
        name="steps",
    )(queries, keys, values)


def last_kernel(x_ref, near_ref, state_ref, near_s, out_ref):
    first = lax.axis_index("grp") * lax.axis_size("seq") + lax.axis_index("seq")
    first = (first * pl.num_programs(0) + pl.program_id(0)) * GROUP
    for c in range(GROUP // BLOCK):
        n = pl.program_id(0) * (GROUP // BLOCK) + c
        row = pl.ds(pl.multiple_of(n * BLOCK, BLOCK), BLOCK)
        place = (first + c * BLOCK + lax.broadcasted_iota(jnp.int32, (BLOCK, HEAD), 0)).astype(F32)
        scale = jnp.sqrt(place + 1.0)
        for h in range(HEADS):
            half = state_ref.shape[0] // HEADS
            state = halves(state_ref[pl.ds(h * half, half)].reshape(HEAD, HEAD) + near_s[n, h])
            out = narrow(*halves(x_ref[row, lanes(h)]), *state)
            out_ref[pl.ds(c * BLOCK, BLOCK), lanes(h)] = (out + near_ref[row, lanes(h)]) * scale


def last(*parts):
    tokens, width = parts[0].shape
    return pl.pallas_call(
        last_kernel,
        grid=(tokens // GROUP,),
        out_shape=jax.ShapeDtypeStruct((tokens, width), F32),
        in_specs=[pl.BlockSpec(memory_space=pltpu.VMEM)] * len(parts),
        out_specs=pl.BlockSpec((GROUP, width), lambda n: (n, 0)),
        compiler_params=pltpu.CompilerParams(vmem_limit_bytes=16 * 2**20),
        name="last",
    )(*parts)


def on_device(queries, keys, values):
    return last(*steps(queries, keys, values, ZDIM))


def solution(mesh):
    return jax.shard_map(
        on_device,
        mesh=mesh,
        in_specs=(P(("grp", "seq"), None), P(("grp", "seq"), None), P(("grp", "seq"), None)),
        out_specs=P(("grp", "seq"), None),
        check_vma=False,
    )
```
